128 devices in a mesh: seq: 4 (over y), mem: 32 (over x, z, core).
Axes of the slice: x: 4, y: 4, z: 4, core: 2. Of those that a mesh axis runs over, the one named last changes fastest.
Arguments:
- queries: bfloat16 [2048, 8192], P(('seq', 'mem')), may hold values from -90 to 90
- probes: int32 [2048, 64, 8], P('seq'), may hold values from 0 to 63, as said below
- keys: bfloat16 [4, 16384, 8192], P('seq', 'mem'), may hold values from -5 to 5
- values: bfloat16 [4, 16384, 8192], P('seq', 'mem'), may hold values from -6 to 6
- w_out: bfloat16 [8192, 8192], P('mem', 'seq'), may hold values from -0.75 to 0.75
Outputs:
- output: bfloat16 [2048, 8192], P(('seq', 'mem'))
The draws below stay inside these ranges and needn't reach their ends.
Inputs may be any that keep to these rules, and one draw needn't show every extreme that they name: `probes`: for each row and head the 8 ids are distinct blocks of the row's group memory.
All inputs are finite; a program needn't handle non-finite values.
Results may differ from the reference program's by a relative error of at most 0.023.
Values may be sent and summed in bfloat16 or wider, within the bound.
No kernel may reach another device: no remote copies, remote signals or barrier semaphores. Data moves between devices by JAX's collectives and lax.ppermute only.
A program may use at most 256 MiB of HBM per device.

```python
import jax
import jax.numpy as jnp
from jax import lax

D = 8192
H = 64
DH = 128
BLOCK = 256
TOPB = 8
Q_DEV = 16
BLK_DEV = 2
MEMORY = 16384
N_SEQ = 4
N_MEM = 32


def probe_table(key):
    row_total = Q_DEV * N_MEM * N_SEQ
    block_count = BLK_DEV * N_MEM
    popular = jax.random.randint(jax.random.fold_in(key, 11), (block_count,), 0, 4) * 400
    noise = jax.random.randint(jax.random.fold_in(key, 12), (row_total, H, block_count), 0, 1024)
    scored = (noise + popular[None, None, :]) * block_count + jnp.arange(block_count, dtype=jnp.int32)
    return lax.top_k(scored, TOPB)[1].astype(jnp.int32)


def key_table(key):
    memory_keys = BLK_DEV * BLOCK * N_MEM
    normal_keys = jnp.clip(jax.random.normal(jax.random.fold_in(key, 21), (N_SEQ, memory_keys, D), jnp.float32), -4.0, 4.0)
    return normal_keys


def draw_probes(key, part):
    return probe_table(key)


def draw_keys(key, part):
    return key_table(key).astype(jnp.bfloat16)


def draw_queries(key, part):
    row_total = Q_DEV * N_MEM * N_SEQ
    drawn_rows = 1.5 * jnp.clip(jax.random.normal(jax.random.fold_in(key, 32), (row_total, D), jnp.float32), -4.0, 4.0)
    return drawn_rows.astype(jnp.bfloat16)


def shard_levels(rng, extent, shards, least, high):
    def one(dim, blocks):
        heights = jax.random.uniform(jax.random.fold_in(jax.random.fold_in(rng, 6), dim), (blocks,), jnp.float32, least / len(shards), high / len(shards))
        return jnp.repeat(jnp.exp(heights), extent[dim] // blocks).reshape((-1,) + (1,) * (len(extent) - dim - 1))

    level = one(*shards[0])
    for cut in shards[1:]:
        level = level * one(*cut)
    return level


def gaussian(rng, shape, deviation, reach, shards=(), kind=jnp.bfloat16):
    factor_of = shard_levels(rng, shape, shards, -0.22, 0.18) if shards else 1.0
    drawn = jax.random.normal(rng, shape, jnp.float32) * deviation * factor_of
    return jnp.minimum(jnp.maximum(drawn, -reach), reach).astype(kind)


def setup_inputs(seed: int = 0) -> dict:
    arg_keys = jax.random.split(jax.random.key(seed), 6)
    queries = draw_queries(jax.random.fold_in(arg_keys[5], 71), 0)
    probes = draw_probes(jax.random.fold_in(arg_keys[5], 71), 0)
    keys = draw_keys(jax.random.fold_in(arg_keys[5], 71), 0)
    values = gaussian(arg_keys[3], (N_SEQ, MEMORY, D), 1.0, 6.0, ((0, 4), (1, 32)))
    w_out = gaussian(arg_keys[4], (D, D), 0.13, 0.75, ((0, 32), (1, 4)))
    return dict(queries=queries, probes=probes, keys=keys, values=values, w_out=w_out)


def attend_head(inputs):
    head_query, head_probe, head_keys, head_values = inputs
    scaling = DH ** -0.5
    chosen_keys = head_keys[head_probe].astype(jnp.float32)
    chosen_values = head_values[head_probe].astype(jnp.float32)
    scores = jnp.einsum("qd,qtkd->qtk", head_query.astype(jnp.float32), chosen_keys) * scaling
    row_top = jnp.max(scores, axis=(1, 2), keepdims=True)
    weights = jnp.exp(scores - row_top)
    totals = jnp.sum(weights, axis=(1, 2))
    rounded = lax.optimization_barrier(weights.astype(jnp.bfloat16)).astype(jnp.float32)
    numerator = jnp.einsum("qtk,qtkd->qd", rounded, chosen_values)
    return numerator / totals[:, None]


def attend_group(inputs):
    group_query, group_probe, group_keys, group_values = inputs
    group_rows = group_query.shape[0]
    block_count = group_keys.shape[0] // BLOCK
    query_heads = jnp.transpose(group_query.reshape(group_rows, H, DH), (1, 0, 2))
    probe_heads = jnp.transpose(group_probe, (1, 0, 2))
    key_heads = jnp.transpose(group_keys.reshape(block_count, BLOCK, H, DH), (2, 0, 1, 3))
    value_heads = jnp.transpose(group_values.reshape(block_count, BLOCK, H, DH), (2, 0, 1, 3))
    result = lax.map(attend_head, (query_heads, probe_heads, key_heads, value_heads))
    return jnp.transpose(result, (1, 0, 2)).reshape(group_rows, H * DH).astype(jnp.bfloat16)


def reference(queries, probes, keys, values, w_out):
    group_rows = Q_DEV * N_MEM
    attended = lax.map(attend_group, (queries.reshape(N_SEQ, group_rows, D), probes.reshape(N_SEQ, group_rows, H, TOPB), keys, values))
    attended = attended.reshape(N_SEQ * group_rows, D)
    return jnp.dot(attended, w_out, preferred_element_type=jnp.float32).astype(jnp.bfloat16)
```

```python
import jax
import jax.numpy as jnp
import numpy as np
from jax import lax
from jax.experimental import pallas as pl
from jax.experimental.pallas import tpu as pltpu
from jax.sharding import Mesh
from jax.sharding import PartitionSpec as P

DH = 128
BLOCK = 256
PAIR = 2 * DH
CHIPS = 16
ROWS = 512
KEYS = 512
STAT = 16
NEG = -1e30
SCALE = DH ** -0.5 * 1.4426950408889634

PLANE = ("x", "z")
SWAP = [(0, 1), (1, 0)]


def split_query_kernel(core_ref, q_ref, own_ref, other_ref):
    first = core_ref[0] == 0
    for i in range(CHIPS):
        even = q_ref[:, 2 * i * PAIR:(2 * i + 1) * PAIR]
        odd = q_ref[:, (2 * i + 1) * PAIR:(2 * i + 2) * PAIR]
        here = pl.ds(i * PAIR, PAIR)
        own_ref[:, here] = jnp.where(first, even, odd)
        other_ref[:, here] = jnp.where(first, odd, even)


def split_query(core, queries):
    rows, width = queries.shape
    half = jax.ShapeDtypeStruct((rows, width // 2), queries.dtype)
    return pl.pallas_call(
        split_query_kernel,
        out_shape=(half, half),
        in_specs=[
            pl.BlockSpec(memory_space=pltpu.SMEM),
            pl.BlockSpec(memory_space=pltpu.VMEM),
        ],
        name="split_query",
    )(core, queries)


def other_half_kernel(core_ref, k_ref, v_ref, ok_ref, ov_ref):
    del core_ref
    ok_ref[...] = k_ref[0]
    ov_ref[...] = v_ref[0]


def other_half(core, keys, values):
    half = jax.ShapeDtypeStruct((KEYS, CHIPS * PAIR), keys.dtype)
    source = pl.BlockSpec((1, KEYS, PAIR), lambda i, core: (0, 0, 2 * i + 1 - core[0]))
    target = pl.BlockSpec((KEYS, PAIR), lambda i, core: (0, i))
    return pl.pallas_call(
        other_half_kernel,
        out_shape=(half, half),
        grid_spec=pltpu.PrefetchScalarGridSpec(
            num_scalar_prefetch=1,
            grid=(CHIPS,),
            in_specs=[source, source],
            out_specs=(target, target),
        ),
        name="other_half",
    )(core, keys, values)


def attend_kernel(info_ref, q_ref, ka_ref, kb_ref, va_ref, vb_ref, probe_ref, out_ref):
    stat_row = lax.broadcasted_iota(jnp.int32, (STAT, ROWS), 0)
    stats = jnp.zeros((STAT, ROWS), jnp.float32)
    for h in range(2):
        lanes = pl.ds(h * DH, DH)
        query = q_ref[:, lanes]
        probe = probe_ref[h]
        scores = []
        probed = []
        top = jnp.full((1, ROWS), NEG, jnp.float32)
        for b in range(4):
            span = pl.ds((b % 2) * BLOCK, BLOCK)
            key = ka_ref[0, span, lanes] if b < 2 else kb_ref[span, lanes]
            s = lax.dot_general(
                key, query, (((1,), (1,)), ((), ())), preferred_element_type=jnp.float32
            )
            hit = jnp.max(jnp.where(probe == info_ref[1 + b], 1.0, 0.0), axis=0, keepdims=True) > 0.5
            top = jnp.maximum(top, jnp.where(hit, jnp.max(s, axis=0, keepdims=True), NEG))
            scores.append(s)
            probed.append(hit)
        top = (top * SCALE).astype(jnp.bfloat16).astype(jnp.float32)
        total = jnp.zeros((1, ROWS), jnp.float32)
        numerator = jnp.zeros((DH, ROWS), jnp.float32)
        for b in range(4):
            span = pl.ds((b % 2) * BLOCK, BLOCK)
            value = va_ref[0, span, lanes] if b < 2 else vb_ref[span, lanes]
            weight = jnp.exp2(scores[b] * SCALE - jnp.where(probed[b], top, -NEG))
            total = total + jnp.sum(weight, axis=0, keepdims=True)
            numerator = numerator + lax.dot_general(
                value, weight.astype(jnp.bfloat16), (((0,), (0,)), ((), ())),
                preferred_element_type=jnp.float32,
            )
        out_ref[0, h * DH:(h + 1) * DH, :] = numerator.astype(jnp.bfloat16)
        high = total.astype(jnp.bfloat16).astype(jnp.float32)
        for j, row in enumerate((top, high, total - high)):
            stats = jnp.where(stat_row == 3 * h + j, row, stats)
    out_ref[0, PAIR:, :] = stats.astype(jnp.bfloat16)


def attend(info, query, keys, other_keys, values, other_values, probes):
    own = pl.BlockSpec((1, KEYS, PAIR), lambda i, info: (0, 0, 2 * i + info[0]))
    half = pl.BlockSpec((KEYS, PAIR), lambda i, info: (0, i))
    return pl.pallas_call(
        attend_kernel,
        out_shape=jax.ShapeDtypeStruct((CHIPS, PAIR + STAT, ROWS), jnp.bfloat16),
        grid_spec=pltpu.PrefetchScalarGridSpec(
            num_scalar_prefetch=1,
            grid=(CHIPS,),
            in_specs=[
                pl.BlockSpec((ROWS, PAIR), lambda i, info: (0, i)),
                own,
                half,
                own,
                half,
                pl.BlockSpec((2, 8, ROWS), lambda i, info: (2 * i + info[0], 0, 0)),
            ],
            out_specs=pl.BlockSpec((1, PAIR + STAT, ROWS), lambda i, info: (i, 0, 0)),
        ),
        compiler_params=pltpu.CompilerParams(vmem_limit_bytes=48 << 20),
        name="attend",
    )(info, query, keys, other_keys, values, other_values, probes)


def combine_kernel(part_ref, out_ref):
    for h in range(2):
        tops = [part_ref[s, PAIR + 3 * h:PAIR + 3 * h + 1, :].astype(jnp.float32) for s in range(CHIPS)]
        top = tops[0]
        for s in range(1, CHIPS):
            top = jnp.maximum(top, tops[s])
        total = jnp.zeros_like(top)
        numerator = jnp.zeros((DH, top.shape[1]), jnp.float32)
        for s in range(CHIPS):
            scale = jnp.exp2(tops[s] - top)
            high = part_ref[s, PAIR + 3 * h + 1:PAIR + 3 * h + 2, :].astype(jnp.float32)
            low = part_ref[s, PAIR + 3 * h + 2:PAIR + 3 * h + 3, :].astype(jnp.float32)
            total = total + scale * (high + low)
            numerator = numerator + scale * part_ref[s, h * DH:(h + 1) * DH, :].astype(jnp.float32)
        out_ref[h * DH:(h + 1) * DH, :] = (numerator / total).astype(jnp.bfloat16)


def combine(parts):
    step = 128
    return pl.pallas_call(
        combine_kernel,
        out_shape=jax.ShapeDtypeStruct((PAIR, ROWS), jnp.bfloat16),
        grid=(ROWS // step,),
        in_specs=[pl.BlockSpec((CHIPS, PAIR + STAT, step), lambda i: (0, 0, i))],
        out_specs=pl.BlockSpec((PAIR, step), lambda i: (0, i)),
        name="combine",
    )(parts)


def shards(queries, probes, keys, values, w_out):
    core = lax.axis_index("c")
    chip = lax.axis_index("x") * 4 + lax.axis_index("z")
    first = core == 0
    core_array = core.astype(jnp.int32).reshape(1)
    own_block = (chip * 2 + core) * 2
    other_block = (chip * 2 + 1 - core) * 2
    info = jnp.stack([core, own_block, own_block + 1, other_block, other_block + 1]).astype(jnp.int32)

    own_query, send_query = split_query(core_array, queries)
    got_query = lax.ppermute(send_query, "c", SWAP)
    chip_query = jnp.where(
        first,
        jnp.concatenate([own_query, got_query], 0),
        jnp.concatenate([got_query, own_query], 0),
    )
    group_query = lax.all_gather(chip_query, PLANE, axis=0, tiled=True)

    send_keys, send_values = other_half(core_array, keys, values)
    other_keys = lax.ppermute(send_keys, "c", SWAP)
    other_values = lax.ppermute(send_values, "c", SWAP)

    w_late, group_query = lax.optimization_barrier((w_out, group_query))
    wide = lax.all_gather(w_late, "y", axis=1, tiled=True)
    half_width = wide.shape[1] // 2
    own_w = lax.dynamic_slice_in_dim(wide, core * half_width, half_width, 1)
    send_w = lax.dynamic_slice_in_dim(wide, (1 - core) * half_width, half_width, 1)
    got_w = lax.ppermute(send_w, "c", SWAP)

    partial = attend(
        info, group_query, keys, other_keys, values, other_values, jnp.transpose(probes, (1, 2, 0))
    )
    parts = lax.all_to_all(partial, PLANE, split_axis=0, concat_axis=0, tiled=True)
    attended = combine(parts)
    got_attended = lax.ppermute(attended, "c", SWAP)

    contract = (((0,), (0,)), ((), ()))
    projected = lax.dot_general(
        jnp.concatenate([attended, got_attended], 0),
        jnp.concatenate([own_w, got_w], 0),
        contract,
        preferred_element_type=jnp.float32,
    ).astype(jnp.bfloat16)
    pieces = lax.all_to_all(
        projected.reshape(CHIPS, ROWS // CHIPS, half_width), PLANE, split_axis=0, concat_axis=0, tiled=True
    )
    summed = jnp.sum(pieces.astype(jnp.float32), axis=0).astype(jnp.bfloat16)
    rows = summed.shape[0] // 2
    own_out = lax.dynamic_slice_in_dim(summed, core * rows, rows, 0)
    send_out = lax.dynamic_slice_in_dim(summed, (1 - core) * rows, rows, 0)
    got_out = lax.ppermute(send_out, "c", SWAP)
    return jnp.where(
        first,
        jnp.concatenate([own_out, got_out], 1),
        jnp.concatenate([got_out, own_out], 1),
    )


def solution(mesh):
    fine = Mesh(mesh.devices.reshape(4, 4, 4, 2), ("y", "x", "z", "c"))
    mem = ("x", "z", "c")
    placed = (
        P(("y",) + mem, None),
        P("y", None, None),
        P("y", mem, None),
        P("y", mem, None),
        P(mem, "y"),
    )
    return jax.shard_map(
        shards, mesh=fine, in_specs=placed, out_specs=P(("y",) + mem, None), check_vma=False
    )
```

```python
import jax
import jax.numpy as jnp
from jax import lax
from jax.experimental import pallas as pl
from jax.experimental.pallas import tpu as pltpu
from jax.sharding import Mesh
from jax.sharding import PartitionSpec as P


DH = 128
BLOCK = 256
PAIR = 2 * DH
SIDE = 4
CHIPS = SIDE * SIDE
ROWS = 512
KEYS = 512
CHIP_ROWS = ROWS // CHIPS
STAT = 16
UNIT = 256
CHUNK = 64
PARTS = 2
PART = PAIR + STAT
NEG = -1e30
SCALE = DH ** -0.5 * 1.4426950408889634

MEM = ("x", "z", "c")
GROUPS = ((0,), (1,), (2, 3))
SHIFTS = (1, 2, 3)
SWAP = [(0, 1), (1, 0)]

CORE = 0
BLOCKS = 1
PAIRS = 5
OTHER_PAIRS = PAIRS + CHIPS
ROW_AT = OTHER_PAIRS + CHIPS
MY_A = ROW_AT + CHIPS
MY_B = MY_A + 1


def shift(axis, step):
    moves = []
    for x in range(SIDE):
        for z in range(SIDE):
            for c in range(2):
                along_z = (axis == "a") == (c == 0)
                to_x = x if along_z else (x + step) % SIDE
                to_z = (z + step) % SIDE if along_z else z
                moves.append(((x * SIDE + z) * 2 + c, (to_x * SIDE + to_z) * 2 + c))
    return moves


def send(value, axis, step):
    return lax.ppermute(value, MEM, shift(axis, step))


def swap(value):
    return lax.ppermute(value, "c", SWAP)


def table_of(x, z, core):
    a = jnp.where(core == 0, z, x)
    b = jnp.where(core == 0, x, z)
    major = jnp.arange(CHIPS, dtype=jnp.int32) // SIDE
    minor = jnp.arange(CHIPS, dtype=jnp.int32) % SIDE

    def chip_at(along_a, along_b, on_core):
        return jnp.where(on_core == 0, along_b * SIDE + along_a, along_a * SIDE + along_b)

    own_block = ((x * SIDE + z) * 2 + core) * 2
    other_block = ((x * SIDE + z) * 2 + 1 - core) * 2
    blocks = jnp.where(jnp.arange(4) < 2, own_block, other_block) + jnp.arange(4) % 2
    pairs = chip_at((a + 1 + major) % SIDE, minor, core)
    other_pairs = chip_at((b + 1 + major) % SIDE, minor, 1 - core)
    row_at = chip_at((a + SIDE - major) % SIDE, minor, core) * CHIP_ROWS
    parts = [core.reshape(1), blocks, pairs, other_pairs, row_at, a.reshape(1), b.reshape(1)]
    return jnp.concatenate([p.astype(jnp.int32) for p in parts])


def whole(count):
    return [pl.BlockSpec(memory_space=pltpu.VMEM)] * count


def split_query_kernel(table, q_ref, own_ref, other_ref):
    first = table[CORE] == 0
    for p in range(CHIPS):
        turned = (p % SIDE) * SIDE + p // SIDE
        zero = q_ref[:, 2 * turned * PAIR:(2 * turned + 1) * PAIR]
        one = q_ref[:, (2 * p + 1) * PAIR:(2 * p + 2) * PAIR]
        here = pl.ds((p % SIDE) * PAIR, PAIR)
        own_ref[p // SIDE, :, here] = jnp.where(first, zero, one)
        other_ref[p // SIDE, :, here] = jnp.where(first, one, zero)


def split_query(table, queries):
    rows = queries.shape[0]
    half = jax.ShapeDtypeStruct((SIDE, rows, SIDE * PAIR), queries.dtype)
    return pl.pallas_call(
        split_query_kernel,
        out_shape=(half, half),
        in_specs=[pl.BlockSpec(memory_space=pltpu.SMEM)] + whole(1),
        name="split_query",
    )(table, queries)


def spread_query_kernel(table, *refs):
    lines, outs = refs[:SIDE], refs[SIDE:]
    a, b = table[MY_A], table[MY_B]
    for t in range(SIDE):
        at = pl.ds(pl.multiple_of(((b + SIDE - t) % SIDE) * CHIP_ROWS, CHIP_ROWS), CHIP_ROWS)
        for g, ks in enumerate(GROUPS):
            for s in range(SIDE):
                for i, k in enumerate(ks):
                    group = (a + s + 1 + k) % SIDE
                    outs[g * SIDE + s][i, at, :] = lines[t][group]


def spread_query(table, lines):
    pieces = [
        jax.ShapeDtypeStruct((len(ks), SIDE * CHIP_ROWS, SIDE * PAIR), lines[0].dtype)
        for ks in GROUPS
        for _ in range(SIDE)
    ]
    return pl.pallas_call(
        spread_query_kernel,
        out_shape=tuple(pieces),
        in_specs=[pl.BlockSpec(memory_space=pltpu.SMEM)] + whole(SIDE),
        name="spread_query",
    )(table, *lines)


def other_half_kernel(table, k_ref, v_ref, ok_ref, ov_ref, stage, in_sem, out_sem):
    other = 1 - table[CORE]

    def fetch(n, i):
        there = pl.ds(pl.multiple_of((2 * i + other) * PAIR, PAIR), PAIR)
        return pltpu.make_async_copy(
            (k_ref, v_ref)[n].at[0, :, there], stage.at[n, :, pl.ds(i * PAIR, PAIR)], in_sem.at[n, i]
        )

    def drain(n, i):
        span = pl.ds(i * (KEYS // CHIPS), KEYS // CHIPS)
        return pltpu.make_async_copy(stage.at[n, span], (ok_ref, ov_ref)[n].at[span], out_sem.at[n, i])

    for n in range(2):
        for i in range(CHIPS):
            fetch(n, i).start()
    for n in range(2):
        for i in range(CHIPS):
            fetch(n, i).wait()
        for i in range(CHIPS):
            drain(n, i).start()
    for n in range(2):
        for i in range(CHIPS):
            drain(n, i).wait()


def other_half(table, keys, values):
    half = jax.ShapeDtypeStruct((KEYS, CHIPS * PAIR), keys.dtype)
    anywhere = pl.BlockSpec(memory_space=pl.ANY)
    return pl.pallas_call(
        other_half_kernel,
        out_shape=(half, half),
        in_specs=[pl.BlockSpec(memory_space=pltpu.SMEM), anywhere, anywhere],
        out_specs=(anywhere, anywhere),
        scratch_shapes=[
            pltpu.VMEM((2, KEYS, CHIPS * PAIR), keys.dtype),
            pltpu.SemaphoreType.DMA((2, CHIPS)),
            pltpu.SemaphoreType.DMA((2, CHIPS)),
        ],
        compiler_params=pltpu.CompilerParams(vmem_limit_bytes=20 << 20),
        name="other_half",
    )(table, keys, values)


def attend_kernel(
    table, q0, q1, q2, q3, ka_ref, kb_ref, va_ref, vb_ref, probe_ref, out_ref, q_ref, s_ref, p_ref
):
    for s, source in enumerate((q0, q1, q2, q3)):
        for b in range(SIDE):
            at = pl.multiple_of(table[ROW_AT + s * SIDE + b], CHIP_ROWS)
            q_ref[pl.ds(at, CHIP_ROWS), :] = source[0, b * CHIP_ROWS:(b + 1) * CHIP_ROWS, :]

    units = [(h, r) for h in range(2) for r in range(ROWS // UNIT)]
    stat_row = lax.broadcasted_iota(jnp.int32, (STAT, UNIT), 0)
    stats = [jnp.zeros((STAT, UNIT), jnp.float32) for _ in range(ROWS // UNIT)]

    def block_tops(u, b):
        h, r = units[u]
        lanes = pl.ds(h * DH, DH)
        span = pl.ds((b % 2) * BLOCK, BLOCK)
        key = ka_ref[0, span, lanes] if b < 2 else kb_ref[span, lanes]
        score = lax.dot_general(
            key, q_ref[r * UNIT:(r + 1) * UNIT, lanes], (((1,), (1,)), ((), ())),
            preferred_element_type=jnp.float32,
        )
        s_ref[u % 2, b] = score
        return jnp.max(score.reshape(-1, 8, UNIT), axis=0)

    def offsets(u, tops):
        h, r = units[u]
        probe = probe_ref[h, :, r * UNIT:(r + 1) * UNIT]
        top = jnp.full((1, UNIT), NEG, jnp.float32)
        hits = []
        for b in range(4):
            hit = jnp.max(jnp.where(probe == table[BLOCKS + b], 1.0, 0.0), axis=0, keepdims=True) > 0.5
            top = jnp.maximum(top, jnp.where(hit, jnp.max(tops[b], axis=0, keepdims=True), NEG))
            hits.append(hit)
        top = (top * SCALE).astype(jnp.bfloat16).astype(jnp.float32)
        return top, [jnp.where(hit, top, -NEG) for hit in hits]

    tops = [block_tops(0, b) for b in range(4)]
    for u, (h, r) in enumerate(units):
        top, offset = offsets(u, tops)
        tops = []
        total = jnp.zeros((8, UNIT), jnp.float32)
        for b in range(4):
            if u + 1 < len(units):
                tops.append(block_tops(u + 1, b))
            for c in range(0, BLOCK, CHUNK):
                weight = jnp.exp2(s_ref[u % 2, b, c:c + CHUNK, :] * SCALE - offset[b])
                total = total + jnp.sum(weight.reshape(-1, 8, UNIT), axis=0)
                p_ref[u % 2, b * BLOCK + c:b * BLOCK + c + CHUNK, :] = weight.astype(jnp.bfloat16)
        lanes = pl.ds(h * DH, DH)
        contract = (((0,), (0,)), ((), ()))
        numerator = lax.dot_general(
            va_ref[0, :, lanes], p_ref[u % 2, :KEYS, :], contract, preferred_element_type=jnp.float32
        ) + lax.dot_general(
            vb_ref[:, lanes], p_ref[u % 2, KEYS:, :], contract, preferred_element_type=jnp.float32
        )
        out_ref[0, h * DH:(h + 1) * DH, r * UNIT:(r + 1) * UNIT] = numerator.astype(jnp.bfloat16)
        total = jnp.sum(total, axis=0, keepdims=True)
        high = total.astype(jnp.bfloat16).astype(jnp.float32)
        for j, row in enumerate((top, high, total - high)):
            stats[r] = jnp.where(stat_row == 3 * h + j, row, stats[r])
    for r, rows in enumerate(stats):
        out_ref[0, PAIR:, r * UNIT:(r + 1) * UNIT] = rows.astype(jnp.bfloat16)


def attend(table, k, place, sources, keys, other_keys, values, other_values, probes):
    def pair(j, table):
        return table[PAIRS + k * SIDE + j]

    own = pl.BlockSpec((1, KEYS, PAIR), lambda j, table: (0, 0, 2 * pair(j, table) + table[CORE]))
    half = pl.BlockSpec((KEYS, PAIR), lambda j, table: (0, pair(j, table)))
    query = pl.BlockSpec((1, SIDE * CHIP_ROWS, PAIR), lambda j, table: (place, 0, j))
    return pl.pallas_call(
        attend_kernel,
        out_shape=jax.ShapeDtypeStruct((SIDE, PART, ROWS), jnp.bfloat16),
        grid_spec=pltpu.PrefetchScalarGridSpec(
            num_scalar_prefetch=1,
            grid=(SIDE,),
            in_specs=[query] * SIDE + [
                own,
                half,
                own,
                half,
                pl.BlockSpec((2, 8, ROWS), lambda j, table: (2 * pair(j, table) + table[CORE], 0, 0)),
            ],
            out_specs=pl.BlockSpec((1, PART, ROWS), lambda j, table: (j, 0, 0)),
            scratch_shapes=[
                pltpu.VMEM((ROWS, PAIR), jnp.bfloat16),
                pltpu.VMEM((2, 4, BLOCK, UNIT), jnp.float32),
                pltpu.VMEM((2, 2 * KEYS, UNIT), jnp.bfloat16),
            ],
        ),
        compiler_params=pltpu.CompilerParams(vmem_limit_bytes=40 << 20),
    )(table, *sources, keys, other_keys, values, other_values, probes)


def merge(parts, h):
    tops = [part[PAIR + 3 * h:PAIR + 3 * h + 1, :].astype(jnp.float32) for part in parts]
    top = tops[0]
    for other in tops[1:]:
        top = jnp.maximum(top, other)
    total = jnp.zeros_like(top)
    numerator = jnp.zeros((DH, top.shape[1]), jnp.float32)
    for part, part_top in zip(parts, tops):
        scale = jnp.exp2(part_top - top)
        high = part[PAIR + 3 * h + 1:PAIR + 3 * h + 2, :].astype(jnp.float32)
        low = part[PAIR + 3 * h + 2:PAIR + 3 * h + 3, :].astype(jnp.float32)
        total = total + scale * (high + low)
        numerator = numerator + scale * part[h * DH:(h + 1) * DH, :].astype(jnp.float32)
    return top, total, numerator


def stat_rows(stats, h, top, total):
    stat_row = lax.broadcasted_iota(jnp.int32, stats.shape, 0)
    high = total.astype(jnp.bfloat16).astype(jnp.float32)
    for j, row in enumerate((top, high, total - high)):
        stats = jnp.where(stat_row == 3 * h + j, row, stats)
    return stats


def combine_kernel(table, *refs):
    ins, outs = refs[:SIDE], refs[SIDE:]
    for t in range(SIDE):
        line = (table[MY_B] + t) % SIDE
        parts = [ref.at[line] for ref in ins]
        stats = jnp.zeros((STAT, ins[0].shape[2]), jnp.float32)
        for h in range(2):
            top, total, numerator = merge(parts, h)
            outs[t][h * DH:(h + 1) * DH, :] = numerator.astype(jnp.bfloat16)
            stats = stat_rows(stats, h, top, total)
        outs[t][PAIR:, :] = stats.astype(jnp.bfloat16)


def combine(table, parts):
    return pl.pallas_call(
        combine_kernel,
        out_shape=(jax.ShapeDtypeStruct((PART, ROWS), jnp.bfloat16),) * SIDE,
        in_specs=[pl.BlockSpec(memory_space=pltpu.SMEM)] + whole(SIDE),
        compiler_params=pltpu.CompilerParams(vmem_limit_bytes=16 << 20),
        name="combine",
    )(table, *parts)


def finish_kernel(table, *refs):
    ins, own_ref, other_ref, rows_ref = refs[:SIDE], refs[SIDE], refs[SIDE + 1], refs[SIDE + 2]
    for h in range(2):
        _, total, numerator = merge(ins, h)
        rows_ref[:, h * DH:(h + 1) * DH] = jnp.transpose(numerator / total).astype(jnp.bfloat16)
    for p in range(CHIPS):
        for ref, at in ((own_ref, PAIRS), (other_ref, OTHER_PAIRS)):
            start = pl.multiple_of(table[at + p] * CHIP_ROWS, CHIP_ROWS)
            ref[p] = rows_ref[pl.ds(start, CHIP_ROWS), :]


def finish(table, parts):
    rows = jax.ShapeDtypeStruct((CHIPS, CHIP_ROWS, PAIR), jnp.bfloat16)
    return pl.pallas_call(
        finish_kernel,
        out_shape=(rows, rows),
        in_specs=[pl.BlockSpec(memory_space=pltpu.SMEM)] + whole(SIDE),
        scratch_shapes=[pltpu.VMEM((ROWS, PAIR), jnp.bfloat16)],
        name="finish",
    )(table, *parts)


def project_kernel(own_ref, got_ref, own_w_ref, got_w_ref, *outs):
    own = own_ref[...].reshape(-1, PAIR)
    got = got_ref[...].reshape(-1, PAIR)
    step = 256
    for n in range(own_w_ref.shape[1] // step):
        lanes = pl.ds(n * step, step)
        result = jnp.dot(own, own_w_ref[:, lanes], preferred_element_type=jnp.float32)
        result = result + jnp.dot(got, got_w_ref[:, lanes], preferred_element_type=jnp.float32)
        result = result.astype(jnp.bfloat16).reshape(len(outs), SIDE, CHIP_ROWS, step)
        for g, out in enumerate(outs):
            out[:, :, lanes] = result[g]


def project(part, own, got, own_w, got_w):
    width = got_w.shape[1] // PARTS
    rows = pl.BlockSpec((CHIPS, CHIP_ROWS, PAIR), lambda i: (0, 0, 0))
    weight = pl.BlockSpec((PAIR, width), lambda i: (0, part), pipeline_mode=pl.Buffered(1))
    out = jax.ShapeDtypeStruct((SIDE, CHIP_ROWS, width), jnp.bfloat16)
    return pl.pallas_call(
        project_kernel,
        out_shape=(out,) * SIDE,
        grid=(1,),
        in_specs=[rows, rows, weight, weight],
        out_specs=(pl.BlockSpec((SIDE, CHIP_ROWS, width), lambda i: (0, 0, 0)),) * SIDE,
        compiler_params=pltpu.CompilerParams(vmem_limit_bytes=24 << 20),
    )(own, got, own_w, got_w)


def add_lines_kernel(table, *refs):
    ins, outs = refs[:SIDE], refs[SIDE:]
    for t in range(SIDE):
        line = (table[MY_B] + t) % SIDE
        total = ins[0][line].astype(jnp.float32)
        for ref in ins[1:]:
            total = total + ref[line].astype(jnp.float32)
        outs[t][...] = total.astype(jnp.bfloat16)


def add_lines(table, parts):
    width = parts[0].shape[2]
    return pl.pallas_call(
        add_lines_kernel,
        out_shape=(jax.ShapeDtypeStruct((CHIP_ROWS, width), jnp.bfloat16),) * SIDE,
        in_specs=[pl.BlockSpec(memory_space=pltpu.SMEM)] + whole(SIDE),
        name="add_lines",
    )(table, *parts)


def add_rows_kernel(table, *refs):
    ins, own_ref, other_ref = refs[:SIDE], refs[SIDE], refs[SIDE + 1]
    rows = CHIP_ROWS // 2
    for ref, core in ((own_ref, table[CORE]), (other_ref, 1 - table[CORE])):
        at = pl.ds(pl.multiple_of(core * rows, rows), rows)
        total = ins[0][at, :].astype(jnp.float32)
        for part in ins[1:]:
            total = total + part[at, :].astype(jnp.float32)
        ref[...] = total.astype(jnp.bfloat16)


def add_rows(table, parts):
    rows = jax.ShapeDtypeStruct((CHIP_ROWS // 2, parts[0].shape[1]), jnp.bfloat16)
    return pl.pallas_call(
        add_rows_kernel,
        out_shape=(rows, rows),
        in_specs=[pl.BlockSpec(memory_space=pltpu.SMEM)] + whole(SIDE),
        name="add_rows",
    )(table, *parts)


def step(queries, probes, keys, values, w_out):
    core = lax.axis_index("c")
    first = core == 0
    table = table_of(lax.axis_index("x"), lax.axis_index("z"), core)
    wide = lax.all_gather(w_out, "y", axis=1, tiled=True)

    own_query, send_query = split_query(table, queries)
    got_query = swap(send_query)
    chip_query = jnp.where(
        first,
        jnp.concatenate([own_query, got_query], 1),
        jnp.concatenate([got_query, own_query], 1),
    )
    lines = [chip_query]
    for s in (1, 2, 3):
        lines.append(send(chip_query, "b", s))

    send_keys, send_values = other_half(table, keys, values)
    other_keys, other_values = swap(send_keys), swap(send_values)

    where = {}
    spread = spread_query(table, lines)
    for g, ks in enumerate(GROUPS):
        sources = [spread[g * SIDE]]
        for s in SHIFTS:
            sources.append(send(spread[g * SIDE + s], "a", s))
        for i, k in enumerate(ks):
            where[k] = (i, sources)

    head_probes = jnp.transpose(probes, (1, 2, 0))
    parts = []
    for k in range(SIDE):
        place, sources = where[k]
        part = attend(
            table, k, place, sources, keys, other_keys, values, other_values, head_probes
        )
        if k < SIDE - 1:
            part = send(part, "a", k + 1)
        parts.append(part)
    wide, parts[-1] = lax.optimization_barrier((wide, parts[-1]))
    width = wide.shape[1] // 2
    send_w = lax.dynamic_slice_in_dim(wide, (1 - core) * width, width, 1)
    own_w = lax.dynamic_slice_in_dim(wide, core * width, width, 1)
    got_w = swap(send_w)
    merged = combine(table, parts)
    passed = [merged[0]]
    for t in (1, 2, 3):
        passed.append(send(merged[t], "b", t))
    own_rows, send_rows = finish(table, passed)
    got_rows = swap(send_rows)

    projected = [project(n, own_rows, got_rows, own_w, got_w) for n in range(PARTS)]
    gathered = []
    for groups in projected:
        arrived = [groups[3]]
        for s in SHIFTS:
            arrived.append(send(groups[s - 1], "a", s))
        gathered.append(arrived)
    own_out, got_out = [], []
    for arrived in gathered:
        summed = add_lines(table, arrived)
        last = [summed[0]]
        for t in SHIFTS:
            last.append(send(summed[t], "b", t))
        kept, given = add_rows(table, last)
        own_out.append(kept)
        got_out.append(swap(given))
    return jnp.where(
        first,
        jnp.concatenate(own_out + got_out, 1),
        jnp.concatenate(got_out + own_out, 1),
    )


def solution(mesh):
    fine = Mesh(mesh.devices.reshape(4, SIDE, SIDE, 2), ("y",) + MEM)
    placed = (
        P(("y",) + MEM, None),
        P("y", None, None),
        P("y", MEM, None),
        P("y", MEM, None),
        P(MEM, "y"),
    )
    return jax.shard_map(
        step, mesh=fine, in_specs=placed, out_specs=P(("y",) + MEM, None), check_vma=False
    )
```

```python
import jax
import jax.numpy as jnp
from jax import lax
from jax.experimental import pallas as pl
from jax.experimental.pallas import tpu as pltpu
from jax.sharding import Mesh
from jax.sharding import PartitionSpec as P


DH = 128
BLOCK = 256
PAIR = 2 * DH
SIDE = 4
CHIPS = SIDE * SIDE
ROWS = 512
KEYS = 512
CHIP_ROWS = ROWS // CHIPS
CORE_ROWS = CHIP_ROWS // 2
STAT = 16
UNIT = 256
CHUNK = 64
PARTS = 2
PART = PAIR + STAT
NEG = -1e30
SCALE = DH ** -0.5 * 1.4426950408889634

MEM = ("x", "z", "c")
GROUPS = ((0,), (1,), (2, 3))
SHIFTS = (1, 2, 3)
SWAP = [(0, 1), (1, 0)]

CORE = 0
BLOCKS = 1
PAIRS = 5
OTHER_PAIRS = PAIRS + CHIPS
ROW_AT = OTHER_PAIRS + CHIPS
MY_A = ROW_AT + CHIPS
MY_B = MY_A + 1


def shift(axis, step):
    moves = []
    for x in range(SIDE):
        for z in range(SIDE):
            for c in range(2):
                along_z = (axis == "a") == (c == 0)
                to_x = x if along_z else (x + step) % SIDE
                to_z = (z + step) % SIDE if along_z else z
                moves.append(((x * SIDE + z) * 2 + c, (to_x * SIDE + to_z) * 2 + c))
    return moves


def send(value, axis, step):
    return lax.ppermute(value, MEM, shift(axis, step))


def swap(value):
    return lax.ppermute(value, "c", SWAP)


def table_of(x, z, core):
    a = jnp.where(core == 0, z, x)
    b = jnp.where(core == 0, x, z)
    major = jnp.arange(CHIPS, dtype=jnp.int32) // SIDE
    minor = jnp.arange(CHIPS, dtype=jnp.int32) % SIDE

    def chip_at(along_a, along_b, on_core):
        return jnp.where(on_core == 0, along_b * SIDE + along_a, along_a * SIDE + along_b)

    own_block = ((x * SIDE + z) * 2 + core) * 2
    other_block = ((x * SIDE + z) * 2 + 1 - core) * 2
    blocks = jnp.where(jnp.arange(4) < 2, own_block, other_block) + jnp.arange(4) % 2
    pairs = chip_at((a + 1 + major) % SIDE, minor, core)
    other_pairs = chip_at((b + 1 + major) % SIDE, minor, 1 - core)
    row_at = chip_at((a + SIDE - major) % SIDE, minor, core) * CHIP_ROWS
    parts = [core.reshape(1), blocks, pairs, other_pairs, row_at, a.reshape(1), b.reshape(1)]
    return jnp.concatenate([p.astype(jnp.int32) for p in parts])


def whole(count):
    return [pl.BlockSpec(memory_space=pltpu.VMEM)] * count


def split_query_kernel(table, q_ref, own_ref, other_ref):
    first = table[CORE] == 0
    for p in range(CHIPS):
        turned = (p % SIDE) * SIDE + p // SIDE
        zero = q_ref[:, 2 * turned * PAIR:(2 * turned + 1) * PAIR]
        one = q_ref[:, (2 * p + 1) * PAIR:(2 * p + 2) * PAIR]
        here = pl.ds((p % SIDE) * PAIR, PAIR)
        own_ref[p // SIDE, :, here] = jnp.where(first, zero, one)
        other_ref[p // SIDE, :, here] = jnp.where(first, one, zero)


def split_query(table, queries):
    rows = queries.shape[0]
    half = jax.ShapeDtypeStruct((SIDE, rows, SIDE * PAIR), queries.dtype)
    return pl.pallas_call(
        split_query_kernel,
        out_shape=(half, half),
        in_specs=[pl.BlockSpec(memory_space=pltpu.SMEM)] + whole(1),
        compiler_params=pltpu.CompilerParams(vmem_limit_bytes=8 << 20),
        name="split_query",
    )(table, queries)


def spread_query_kernel(table, *refs):
    lines, outs = refs[:SIDE], refs[SIDE:]
    a, b = table[MY_A], table[MY_B]
    for t in range(SIDE):
        at = pl.ds(pl.multiple_of(((b + SIDE - t) % SIDE) * CHIP_ROWS, CHIP_ROWS), CHIP_ROWS)
        for g, ks in enumerate(GROUPS):
            for s in range(SIDE):
                for i, k in enumerate(ks):
                    group = (a + s + 1 + k) % SIDE
                    outs[g * SIDE + s][i, at, :] = lines[t][group]


def spread_query(table, lines):
    pieces = [
        jax.ShapeDtypeStruct((len(ks), SIDE * CHIP_ROWS, SIDE * PAIR), lines[0].dtype)
        for ks in GROUPS
        for _ in range(SIDE)
    ]
    return pl.pallas_call(
        spread_query_kernel,
        out_shape=tuple(pieces),
        in_specs=[pl.BlockSpec(memory_space=pltpu.SMEM)] + whole(SIDE),
        compiler_params=pltpu.CompilerParams(vmem_limit_bytes=16 << 20),
        name="spread_query",
    )(table, *lines)


def other_half_kernel(table, *refs):
    del table
    ins, outs = refs[:2 * SIDE], refs[2 * SIDE:]
    for n, out in enumerate(outs):
        for j in range(SIDE):
            out[:, j * PAIR:(j + 1) * PAIR] = ins[n * SIDE + j][0]


def other_half(table, keys, values):
    half = jax.ShapeDtypeStruct((KEYS, CHIPS * PAIR), keys.dtype)

    def source(j):
        return pl.BlockSpec(
            (1, KEYS, PAIR), lambda i, table: (0, 0, 2 * (i * SIDE + j) + 1 - table[CORE])
        )

    return pl.pallas_call(
        other_half_kernel,
        out_shape=(half, half),
        grid_spec=pltpu.PrefetchScalarGridSpec(
            num_scalar_prefetch=1,
            grid=(SIDE,),
            in_specs=[source(j) for j in range(SIDE)] * 2,
            out_specs=(pl.BlockSpec((KEYS, SIDE * PAIR), lambda i, table: (0, i)),) * 2,
        ),
        name="other_half",
    )(table, *[keys] * SIDE, *[values] * SIDE)


def attend_kernel(
    table, q0, q1, q2, q3, ka_ref, kb_ref, va_ref, vb_ref, probe_ref, out_ref, q_ref, s_ref, p_ref
):
    for s, source in enumerate((q0, q1, q2, q3)):
        for b in range(SIDE):
            at = pl.multiple_of(table[ROW_AT + s * SIDE + b], CHIP_ROWS)
            q_ref[pl.ds(at, CHIP_ROWS), :] = source[0, b * CHIP_ROWS:(b + 1) * CHIP_ROWS, :]

    units = [(h, r) for h in range(2) for r in range(ROWS // UNIT)]
    stat_row = lax.broadcasted_iota(jnp.int32, (STAT, UNIT), 0)
    stats = [jnp.zeros((STAT, UNIT), jnp.float32) for _ in range(ROWS // UNIT)]

    def block_tops(u, b):
        h, r = units[u]
        lanes = pl.ds(h * DH, DH)
        span = pl.ds((b % 2) * BLOCK, BLOCK)
        key = ka_ref[0, span, lanes] if b < 2 else kb_ref[span, lanes]
        score = lax.dot_general(
            key, q_ref[r * UNIT:(r + 1) * UNIT, lanes], (((1,), (1,)), ((), ())),
            preferred_element_type=jnp.float32,
        )
        s_ref[u % 2, b] = score
        return jnp.max(score.reshape(-1, 8, UNIT), axis=0)

    def offsets(u, tops):
        h, r = units[u]
        probe = probe_ref[h, :, r * UNIT:(r + 1) * UNIT]
        top = jnp.full((1, UNIT), NEG, jnp.float32)
        hits = []
        for b in range(4):
            hit = jnp.max(jnp.where(probe == table[BLOCKS + b], 1.0, 0.0), axis=0, keepdims=True) > 0.5
            top = jnp.maximum(top, jnp.where(hit, jnp.max(tops[b], axis=0, keepdims=True), NEG))
            hits.append(hit)
        top = (top * SCALE).astype(jnp.bfloat16).astype(jnp.float32)
        return top, [jnp.where(hit, top, -NEG) for hit in hits]

    tops = [block_tops(0, b) for b in range(4)]
    for u, (h, r) in enumerate(units):
        top, offset = offsets(u, tops)
        tops = []
        total = jnp.zeros((8, UNIT), jnp.float32)
        for b in range(4):
            if u + 1 < len(units):
                tops.append(block_tops(u + 1, b))
            for c in range(0, BLOCK, CHUNK):
                weight = jnp.exp2(s_ref[u % 2, b, c:c + CHUNK, :] * SCALE - offset[b])
                total = total + jnp.sum(weight.reshape(-1, 8, UNIT), axis=0)
                p_ref[u % 2, b * BLOCK + c:b * BLOCK + c + CHUNK, :] = weight.astype(jnp.bfloat16)
        lanes = pl.ds(h * DH, DH)
        contract = (((0,), (0,)), ((), ()))
        numerator = lax.dot_general(
            va_ref[0, :, lanes], p_ref[u % 2, :KEYS, :], contract, preferred_element_type=jnp.float32
        ) + lax.dot_general(
            vb_ref[:, lanes], p_ref[u % 2, KEYS:, :], contract, preferred_element_type=jnp.float32
        )
        out_ref[0, h * DH:(h + 1) * DH, r * UNIT:(r + 1) * UNIT] = numerator.astype(jnp.bfloat16)
        total = jnp.sum(total, axis=0, keepdims=True)
        high = total.astype(jnp.bfloat16).astype(jnp.float32)
        for j, row in enumerate((top, high, total - high)):
            stats[r] = jnp.where(stat_row == 3 * h + j, row, stats[r])
    for r, rows in enumerate(stats):
        out_ref[0, PAIR:, r * UNIT:(r + 1) * UNIT] = rows.astype(jnp.bfloat16)


def attend(table, k, place, sources, keys, other_keys, values, other_values, probes):
    def pair(j, table):
        return table[PAIRS + k * SIDE + j]

    own = pl.BlockSpec((1, KEYS, PAIR), lambda j, table: (0, 0, 2 * pair(j, table) + table[CORE]))
    half = pl.BlockSpec((KEYS, PAIR), lambda j, table: (0, pair(j, table)))
    query = pl.BlockSpec((1, SIDE * CHIP_ROWS, PAIR), lambda j, table: (place, 0, j))
    return pl.pallas_call(
        attend_kernel,
        out_shape=jax.ShapeDtypeStruct((SIDE, PART, ROWS), jnp.bfloat16),
        grid_spec=pltpu.PrefetchScalarGridSpec(
            num_scalar_prefetch=1,
            grid=(SIDE,),
            in_specs=[query] * SIDE + [
                own,
                half,
                own,
                half,
                pl.BlockSpec((2, 8, ROWS), lambda j, table: (2 * pair(j, table) + table[CORE], 0, 0)),
            ],
            out_specs=pl.BlockSpec((1, PART, ROWS), lambda j, table: (j, 0, 0)),
            scratch_shapes=[
                pltpu.VMEM((ROWS, PAIR), jnp.bfloat16),
                pltpu.VMEM((2, 4, BLOCK, UNIT), jnp.float32),
                pltpu.VMEM((2, 2 * KEYS, UNIT), jnp.bfloat16),
            ],
        ),
        compiler_params=pltpu.CompilerParams(vmem_limit_bytes=40 << 20),
    )(table, *sources, keys, other_keys, values, other_values, probes)


def merge(parts, h):
    tops = [part[PAIR + 3 * h:PAIR + 3 * h + 1, :].astype(jnp.float32) for part in parts]
    top = tops[0]
    for other in tops[1:]:
        top = jnp.maximum(top, other)
    total = jnp.zeros_like(top)
    numerator = jnp.zeros((DH, top.shape[1]), jnp.float32)
    for part, part_top in zip(parts, tops):
        scale = jnp.exp2(part_top - top)
        high = part[PAIR + 3 * h + 1:PAIR + 3 * h + 2, :].astype(jnp.float32)
        low = part[PAIR + 3 * h + 2:PAIR + 3 * h + 3, :].astype(jnp.float32)
        total = total + scale * (high + low)
        numerator = numerator + scale * part[h * DH:(h + 1) * DH, :].astype(jnp.float32)
    return top, total, numerator


def stat_rows(stats, h, top, total):
    stat_row = lax.broadcasted_iota(jnp.int32, stats.shape, 0)
    high = total.astype(jnp.bfloat16).astype(jnp.float32)
    for j, row in enumerate((top, high, total - high)):
        stats = jnp.where(stat_row == 3 * h + j, row, stats)
    return stats


def combine_kernel(table, *refs):
    ins, outs = refs[:SIDE], refs[SIDE:]
    for t in range(SIDE):
        line = (table[MY_B] + t) % SIDE
        parts = [ref.at[line] for ref in ins]
        stats = jnp.zeros((STAT, ins[0].shape[2]), jnp.float32)
        for h in range(2):
            top, total, numerator = merge(parts, h)
            outs[t][h * DH:(h + 1) * DH, :] = numerator.astype(jnp.bfloat16)
            stats = stat_rows(stats, h, top, total)
        outs[t][PAIR:, :] = stats.astype(jnp.bfloat16)


def combine(table, parts):
    return pl.pallas_call(
        combine_kernel,
        out_shape=(jax.ShapeDtypeStruct((PART, ROWS), jnp.bfloat16),) * SIDE,
        in_specs=[pl.BlockSpec(memory_space=pltpu.SMEM)] + whole(SIDE),
        compiler_params=pltpu.CompilerParams(vmem_limit_bytes=16 << 20),
        name="combine",
    )(table, *parts)


def finish_kernel(table, *refs):
    ins, own_ref, other_ref, rows_ref = refs[:SIDE], refs[SIDE], refs[SIDE + 1], refs[SIDE + 2]
    for h in range(2):
        _, total, numerator = merge(ins, h)
        rows_ref[:, h * DH:(h + 1) * DH] = jnp.transpose(numerator / total).astype(jnp.bfloat16)
    for ref, at, core in ((own_ref, PAIRS, table[CORE]), (other_ref, OTHER_PAIRS, 1 - table[CORE])):
        for p in range(CHIPS):
            start = pl.multiple_of(table[at + p] * CHIP_ROWS + core * CORE_ROWS, CORE_ROWS)
            ref[p] = rows_ref[pl.ds(start, CORE_ROWS), :]


def finish(table, parts):
    rows = jax.ShapeDtypeStruct((CHIPS, CORE_ROWS, PAIR), jnp.bfloat16)
    return pl.pallas_call(
        finish_kernel,
        out_shape=(rows, rows),
        in_specs=[pl.BlockSpec(memory_space=pltpu.SMEM)] + whole(SIDE),
        scratch_shapes=[pltpu.VMEM((ROWS, PAIR), jnp.bfloat16)],
        compiler_params=pltpu.CompilerParams(vmem_limit_bytes=12 << 20),
        name="finish",
    )(table, *parts)


def project_kernel(own_ref, got_ref, own_w_ref, got_w_ref, *outs):
    own = own_ref[...].reshape(-1, PAIR)
    got = got_ref[...].reshape(-1, PAIR)
    step = 256
    for n in range(own_w_ref.shape[1] // step):
        lanes = pl.ds(n * step, step)
        result = jnp.dot(own, own_w_ref[:, lanes], preferred_element_type=jnp.float32)
        result = result + jnp.dot(got, got_w_ref[:, lanes], preferred_element_type=jnp.float32)
        result = result.astype(jnp.bfloat16).reshape(len(outs), SIDE, CORE_ROWS, step)
        for g, out in enumerate(outs):
            out[:, :, lanes] = result[g]


def project(part, own, got, own_w, got_w):
    width = got_w.shape[1] // PARTS
    rows = pl.BlockSpec((CHIPS, CORE_ROWS, PAIR), lambda i: (0, 0, 0))
    weight = pl.BlockSpec((PAIR, width), lambda i: (0, part), pipeline_mode=pl.Buffered(1))
    out = jax.ShapeDtypeStruct((SIDE, CORE_ROWS, width), jnp.bfloat16)
    return pl.pallas_call(
        project_kernel,
        out_shape=(out,) * SIDE,
        grid=(1,),
        in_specs=[rows, rows, weight, weight],
        out_specs=(pl.BlockSpec((SIDE, CORE_ROWS, width), lambda i: (0, 0, 0)),) * SIDE,
        compiler_params=pltpu.CompilerParams(vmem_limit_bytes=24 << 20),
    )(own, got, own_w, got_w)


def add_lines_kernel(table, *refs):
    ins, outs = refs[:SIDE], refs[SIDE:]
    for t in range(SIDE):
        line = (table[MY_B] + t) % SIDE
        total = ins[0][line].astype(jnp.float32)
        for ref in ins[1:]:
            total = total + ref[line].astype(jnp.float32)
        outs[t][...] = total.astype(jnp.bfloat16)


def add_lines(table, parts):
    width = parts[0].shape[2]
    return pl.pallas_call(
        add_lines_kernel,
        out_shape=(jax.ShapeDtypeStruct((CORE_ROWS, width), jnp.bfloat16),) * SIDE,
        in_specs=[pl.BlockSpec(memory_space=pltpu.SMEM)] + whole(SIDE),
        compiler_params=pltpu.CompilerParams(vmem_limit_bytes=8 << 20),
        name="add_lines",
    )(table, *parts)


def add_rows_kernel(*refs):
    out_ref = refs[-1]
    width = out_ref.shape[1] // PARTS
    for n in range(PARTS):
        lanes = pl.ds(n * width, width)
        ins = refs[n * SIDE:(n + 1) * SIDE]
        total = ins[0][...].astype(jnp.float32)
        for part in ins[1:]:
            total = total + part[...].astype(jnp.float32)
        out_ref[:, lanes] = total.astype(jnp.bfloat16)


def add_rows(parts):
    rows, width = parts[0].shape
    return pl.pallas_call(
        add_rows_kernel,
        out_shape=jax.ShapeDtypeStruct((rows, PARTS * width), jnp.bfloat16),
        in_specs=whole(len(parts)),
        compiler_params=pltpu.CompilerParams(vmem_limit_bytes=8 << 20),
        name="add_rows",
    )(*parts)


def step(queries, probes, keys, values, w_out):
    core = lax.axis_index("c")
    first = core == 0
    table = table_of(lax.axis_index("x"), lax.axis_index("z"), core)
    wide = lax.all_gather(w_out, "y", axis=1, tiled=True)

    own_query, send_query = split_query(table, queries)
    got_query = swap(send_query)
    chip_query = jnp.where(
        first,
        jnp.concatenate([own_query, got_query], 1),
        jnp.concatenate([got_query, own_query], 1),
    )
    lines = [chip_query]
    for s in (1, 2, 3):
        lines.append(send(chip_query, "b", s))

    send_keys, send_values = other_half(table, keys, values)
    other_keys, other_values = swap(send_keys), swap(send_values)

    where = {}
    spread = spread_query(table, lines)
    for g, ks in enumerate(GROUPS):
        sources = [spread[g * SIDE]]
        for s in SHIFTS:
            sources.append(send(spread[g * SIDE + s], "a", s))
        for i, k in enumerate(ks):
            where[k] = (i, sources)

    head_probes = jnp.transpose(probes, (1, 2, 0))
    parts = []
    for k in range(SIDE):
        place, sources = where[k]
        part = attend(
            table, k, place, sources, keys, other_keys, values, other_values, head_probes
        )
        if k < SIDE - 1:
            part = send(part, "a", k + 1)
        parts.append(part)
    wide, parts[-1] = lax.optimization_barrier((wide, parts[-1]))
    got_wide = swap(wide)
    merged = combine(table, parts)
    passed = [merged[0]]
    for t in (1, 2, 3):
        passed.append(send(merged[t], "b", t))
    own_rows, send_rows = finish(table, passed)
    got_rows = swap(send_rows)

    projected = [project(n, own_rows, got_rows, wide, got_wide) for n in range(PARTS)]
    gathered = []
    for groups in projected:
        arrived = [groups[3]]
        for s in SHIFTS:
            arrived.append(send(groups[s - 1], "a", s))
        gathered.append(arrived)
    last = []
    for arrived in gathered:
        summed = add_lines(table, arrived)
        last.append(summed[0])
        for t in SHIFTS:
            last.append(send(summed[t], "b", t))
    return add_rows(last)


def solution(mesh):
    fine = Mesh(mesh.devices.reshape(4, SIDE, SIDE, 2), ("y",) + MEM)
    placed = (
        P(("y",) + MEM, None),
        P("y", None, None),
        P("y", MEM, None),
        P("y", MEM, None),
        P(MEM, "y"),
    )
    return jax.shard_map(
        step, mesh=fine, in_specs=placed, out_specs=P(("y",) + MEM, None), check_vma=False
    )
```

```python
import jax
import jax.numpy as jnp
from jax import lax
from jax.experimental import pallas as pl
from jax.experimental.pallas import tpu as pltpu
from jax.sharding import Mesh
from jax.sharding import PartitionSpec as P


DH = 128
BLOCK = 256
PAIR = 2 * DH
SIDE = 4
CHIPS = SIDE * SIDE
ROWS = 512
KEYS = 512
CHIP_ROWS = ROWS // CHIPS
CORE_ROWS = CHIP_ROWS // 2
STAT = 16
UNIT = 256
CHUNK = 64
PARTS = 2
PART = PAIR + STAT
NEG = -1e30
SCALE = DH ** -0.5 * 1.4426950408889634

MEM = ("x", "z", "c")
GROUPS = ((0, 1), (2, 3))
CALLS = ((0, 0, 4), (1, 0, 4), (2, 0, 2), (2, 2, 2), (3, 0, 4))
SHIFTS = (1, 2, 3)
SWAP = [(0, 1), (1, 0)]

CORE = 0
BLOCKS = 1
PAIRS = 5
OTHER_PAIRS = PAIRS + CHIPS
ROW_AT = OTHER_PAIRS + CHIPS
MY_A = ROW_AT + CHIPS
MY_B = MY_A + 1


def shift(axis, step):
    moves = []
    for x in range(SIDE):
        for z in range(SIDE):
            for c in range(2):
                along_z = (axis == "a") == (c == 0)
                to_x = x if along_z else (x + step) % SIDE
                to_z = (z + step) % SIDE if along_z else z
                moves.append(((x * SIDE + z) * 2 + c, (to_x * SIDE + to_z) * 2 + c))
    return moves


def send(value, axis, step):
    return lax.ppermute(value, MEM, shift(axis, step))


def swap(value):
    return lax.ppermute(value, "c", SWAP)


def table_of(x, z, core):
    a = jnp.where(core == 0, z, x)
    b = jnp.where(core == 0, x, z)
    major = jnp.arange(CHIPS, dtype=jnp.int32) // SIDE
    minor = jnp.arange(CHIPS, dtype=jnp.int32) % SIDE

    def chip_at(along_a, along_b, on_core):
        return jnp.where(on_core == 0, along_b * SIDE + along_a, along_a * SIDE + along_b)

    own_block = ((x * SIDE + z) * 2 + core) * 2
    other_block = ((x * SIDE + z) * 2 + 1 - core) * 2
    blocks = jnp.where(jnp.arange(4) < 2, own_block, other_block) + jnp.arange(4) % 2
    pairs = chip_at((a + 1 + major) % SIDE, (b + minor) % SIDE, core)
    other_pairs = chip_at((b + 1 + major) % SIDE, (a + minor) % SIDE, 1 - core)
    row_at = chip_at((a + SIDE - major) % SIDE, minor, core) * CHIP_ROWS
    parts = [core.reshape(1), blocks, pairs, other_pairs, row_at, a.reshape(1), b.reshape(1)]
    return jnp.concatenate([p.astype(jnp.int32) for p in parts])


def whole(count):
    return [pl.BlockSpec(memory_space=pltpu.VMEM)] * count


def split_query_kernel(table, q_ref, own_ref, other_ref):
    first = table[CORE] == 0
    for p in range(CHIPS):
        turned = (p % SIDE) * SIDE + p // SIDE
        zero = q_ref[:, 2 * turned * PAIR:(2 * turned + 1) * PAIR]
        one = q_ref[:, (2 * p + 1) * PAIR:(2 * p + 2) * PAIR]
        here = pl.ds((p % SIDE) * PAIR, PAIR)
        own_ref[p // SIDE, :, here] = jnp.where(first, zero, one)
        other_ref[p // SIDE, :, here] = jnp.where(first, one, zero)


def split_query(table, queries):
    rows = queries.shape[0]
    half = jax.ShapeDtypeStruct((SIDE, rows, SIDE * PAIR), queries.dtype)
    return pl.pallas_call(
        split_query_kernel,
        out_shape=(half, half),
        in_specs=[pl.BlockSpec(memory_space=pltpu.SMEM)] + whole(1),
        compiler_params=pltpu.CompilerParams(vmem_limit_bytes=8 << 20),
        name="split_query",
    )(table, queries)


def spread_query_kernel(table, *refs):
    lines, outs = refs[:SIDE], refs[SIDE:]
    a, b = table[MY_A], table[MY_B]
    for t in range(SIDE):
        at = pl.ds(pl.multiple_of(((b + SIDE - t) % SIDE) * CHIP_ROWS, CHIP_ROWS), CHIP_ROWS)
        for g, ks in enumerate(GROUPS):
            for s in range(SIDE):
                for i, k in enumerate(ks):
                    group = (a + s + 1 + k) % SIDE
                    outs[g * SIDE + s][i, at, :] = lines[t][group]


def spread_query(table, lines):
    pieces = [
        jax.ShapeDtypeStruct((len(ks), SIDE * CHIP_ROWS, SIDE * PAIR), lines[0].dtype)
        for ks in GROUPS
        for _ in range(SIDE)
    ]
    return pl.pallas_call(
        spread_query_kernel,
        out_shape=tuple(pieces),
        in_specs=[pl.BlockSpec(memory_space=pltpu.SMEM)] + whole(SIDE),
        compiler_params=pltpu.CompilerParams(vmem_limit_bytes=16 << 20),
        name="spread_query",
    )(table, *lines)


def other_half_kernel(table, *refs):
    del table
    ins, outs = refs[:2 * SIDE], refs[2 * SIDE:]
    for n, out in enumerate(outs):
        for j in range(SIDE):
            out[:, j * PAIR:(j + 1) * PAIR] = ins[n * SIDE + j][0]


def other_half(table, keys, values):
    half = jax.ShapeDtypeStruct((KEYS, CHIPS * PAIR), keys.dtype)

    def source(j):
        return pl.BlockSpec(
            (1, KEYS, PAIR), lambda i, table: (0, 0, 2 * (i * SIDE + j) + 1 - table[CORE])
        )

    return pl.pallas_call(
        other_half_kernel,
        out_shape=(half, half),
        grid_spec=pltpu.PrefetchScalarGridSpec(
            num_scalar_prefetch=1,
            grid=(SIDE,),
            in_specs=[source(j) for j in range(SIDE)] * 2,
            out_specs=(pl.BlockSpec((KEYS, SIDE * PAIR), lambda i, table: (0, i)),) * 2,
        ),
        name="other_half",
    )(table, *[keys] * SIDE, *[values] * SIDE)


def attend_kernel(
    table, q0, q1, q2, q3, ka_ref, kb_ref, va_ref, vb_ref, probe_ref, out_ref, q_ref, s_ref, p_ref
):
    for s, source in enumerate((q0, q1, q2, q3)):
        for b in range(SIDE):
            at = pl.multiple_of(table[ROW_AT + s * SIDE + b], CHIP_ROWS)
            q_ref[pl.ds(at, CHIP_ROWS), :] = source[0, b * CHIP_ROWS:(b + 1) * CHIP_ROWS, :]

    units = [(h, r) for h in range(2) for r in range(ROWS // UNIT)]
    stat_row = lax.broadcasted_iota(jnp.int32, (STAT, UNIT), 0)
    stats = [jnp.zeros((STAT, UNIT), jnp.float32) for _ in range(ROWS // UNIT)]

    def block_tops(u, b):
        h, r = units[u]
        lanes = pl.ds(h * DH, DH)
        span = pl.ds((b % 2) * BLOCK, BLOCK)
        key = ka_ref[0, span, lanes] if b < 2 else kb_ref[span, lanes]
        score = lax.dot_general(
            key, q_ref[r * UNIT:(r + 1) * UNIT, lanes], (((1,), (1,)), ((), ())),
            preferred_element_type=jnp.float32,
        )
        s_ref[u % 2, b] = score
        return jnp.max(score.reshape(-1, 8, UNIT), axis=0)

    def offsets(u, tops):
        h, r = units[u]
        probe = probe_ref[h, :, r * UNIT:(r + 1) * UNIT]
        top = jnp.full((1, UNIT), NEG, jnp.float32)
        hits = []
        for b in range(4):
            hit = jnp.max(jnp.where(probe == table[BLOCKS + b], 1.0, 0.0), axis=0, keepdims=True) > 0.5
            top = jnp.maximum(top, jnp.where(hit, jnp.max(tops[b], axis=0, keepdims=True), NEG))
            hits.append(hit)
        top = (top * SCALE).astype(jnp.bfloat16).astype(jnp.float32)
        return top, [jnp.where(hit, top, -NEG) for hit in hits]

    tops = [block_tops(0, b) for b in range(4)]
    for u, (h, r) in enumerate(units):
        top, offset = offsets(u, tops)
        tops = []
        total = jnp.zeros((8, UNIT), jnp.float32)
        for b in range(4):
            if u + 1 < len(units):
                tops.append(block_tops(u + 1, b))
            for c in range(0, BLOCK, CHUNK):
                weight = jnp.exp2(s_ref[u % 2, b, c:c + CHUNK, :] * SCALE - offset[b])
                total = total + jnp.sum(weight.reshape(-1, 8, UNIT), axis=0)
                p_ref[u % 2, b * BLOCK + c:b * BLOCK + c + CHUNK, :] = weight.astype(jnp.bfloat16)
        lanes = pl.ds(h * DH, DH)
        contract = (((0,), (0,)), ((), ()))
        numerator = lax.dot_general(
            va_ref[0, :, lanes], p_ref[u % 2, :KEYS, :], contract, preferred_element_type=jnp.float32
        ) + lax.dot_general(
            vb_ref[:, lanes], p_ref[u % 2, KEYS:, :], contract, preferred_element_type=jnp.float32
        )
        out_ref[0, h * DH:(h + 1) * DH, r * UNIT:(r + 1) * UNIT] = numerator.astype(jnp.bfloat16)
        total = jnp.sum(total, axis=0, keepdims=True)
        high = total.astype(jnp.bfloat16).astype(jnp.float32)
        for j, row in enumerate((top, high, total - high)):
            stats[r] = jnp.where(stat_row == 3 * h + j, row, stats[r])
    for r, rows in enumerate(stats):
        out_ref[0, PAIR:, r * UNIT:(r + 1) * UNIT] = rows.astype(jnp.bfloat16)


def attend(table, k, start, count, place, sources, keys, other_keys, values, other_values, probes):
    def pair(j, table):
        return table[PAIRS + k * SIDE + start + j]

    own = pl.BlockSpec((1, KEYS, PAIR), lambda j, table: (0, 0, 2 * pair(j, table) + table[CORE]))
    half = pl.BlockSpec((KEYS, PAIR), lambda j, table: (0, pair(j, table)))
    query = pl.BlockSpec((1, SIDE * CHIP_ROWS, PAIR), lambda j, table: (place, 0, (table[MY_B] + start + j) % SIDE))
    return pl.pallas_call(
        attend_kernel,
        out_shape=jax.ShapeDtypeStruct((count, PART, ROWS), jnp.bfloat16),
        grid_spec=pltpu.PrefetchScalarGridSpec(
            num_scalar_prefetch=1,
            grid=(count,),
            in_specs=[query] * SIDE + [
                own,
                half,
                own,
                half,
                pl.BlockSpec((2, 8, ROWS), lambda j, table: (2 * pair(j, table) + table[CORE], 0, 0)),
            ],
            out_specs=pl.BlockSpec((1, PART, ROWS), lambda j, table: (j, 0, 0)),
            scratch_shapes=[
                pltpu.VMEM((ROWS, PAIR), jnp.bfloat16),
                pltpu.VMEM((2, 4, BLOCK, UNIT), jnp.float32),
                pltpu.VMEM((2, 2 * KEYS, UNIT), jnp.bfloat16),
            ],
        ),
        compiler_params=pltpu.CompilerParams(vmem_limit_bytes=40 << 20),
    )(table, *sources, keys, other_keys, values, other_values, probes)


def merge(parts, h):
    tops = [part[PAIR + 3 * h:PAIR + 3 * h + 1, :].astype(jnp.float32) for part in parts]
    top = tops[0]
    for other in tops[1:]:
        top = jnp.maximum(top, other)
    total = jnp.zeros_like(top)
    numerator = jnp.zeros((DH, top.shape[1]), jnp.float32)
    for part, part_top in zip(parts, tops):
        scale = jnp.exp2(part_top - top)
        high = part[PAIR + 3 * h + 1:PAIR + 3 * h + 2, :].astype(jnp.float32)
        low = part[PAIR + 3 * h + 2:PAIR + 3 * h + 3, :].astype(jnp.float32)
        total = total + scale * (high + low)
        numerator = numerator + scale * part[h * DH:(h + 1) * DH, :].astype(jnp.float32)
    return top, total, numerator


def stat_rows(stats, h, top, total):
    stat_row = lax.broadcasted_iota(jnp.int32, stats.shape, 0)
    high = total.astype(jnp.bfloat16).astype(jnp.float32)
    for j, row in enumerate((top, high, total - high)):
        stats = jnp.where(stat_row == 3 * h + j, row, stats)
    return stats


def combine_kernel(*refs):
    ins, outs = refs[:-SIDE], refs[-SIDE:]
    lines = [[] for _ in range(SIDE)]
    at = 0
    for ref in ins:
        for i in range(ref.shape[0]):
            lines[at % SIDE].append(ref.at[i])
            at += 1
    for parts, out in zip(lines, outs):
        stats = jnp.zeros((STAT, ROWS), jnp.float32)
        for h in range(2):
            top, total, numerator = merge(parts, h)
            out[h * DH:(h + 1) * DH, :] = numerator.astype(jnp.bfloat16)
            stats = stat_rows(stats, h, top, total)
        out[PAIR:, :] = stats.astype(jnp.bfloat16)


def combine(parts):
    return pl.pallas_call(
        combine_kernel,
        out_shape=(jax.ShapeDtypeStruct((PART, ROWS), jnp.bfloat16),) * SIDE,
        in_specs=whole(len(parts)),
        compiler_params=pltpu.CompilerParams(vmem_limit_bytes=16 << 20),
        name="combine",
    )(*parts)


def finish_kernel(table, *refs):
    ins, own_ref, other_ref, rows_ref = refs[:SIDE], refs[SIDE], refs[SIDE + 1], refs[SIDE + 2]
    for h in range(2):
        _, total, numerator = merge(ins, h)
        rows_ref[:, h * DH:(h + 1) * DH] = jnp.transpose(numerator / total).astype(jnp.bfloat16)
    for ref, at, core in ((own_ref, PAIRS, table[CORE]), (other_ref, OTHER_PAIRS, 1 - table[CORE])):
        for p in range(CHIPS):
            start = pl.multiple_of(table[at + p] * CHIP_ROWS + core * CORE_ROWS, CORE_ROWS)
            ref[p] = rows_ref[pl.ds(start, CORE_ROWS), :]


def finish(table, parts):
    rows = jax.ShapeDtypeStruct((CHIPS, CORE_ROWS, PAIR), jnp.bfloat16)
    return pl.pallas_call(
        finish_kernel,
        out_shape=(rows, rows),
        in_specs=[pl.BlockSpec(memory_space=pltpu.SMEM)] + whole(SIDE),
        scratch_shapes=[pltpu.VMEM((ROWS, PAIR), jnp.bfloat16)],
        compiler_params=pltpu.CompilerParams(vmem_limit_bytes=12 << 20),
        name="finish",
    )(table, *parts)


def project_kernel(own_ref, got_ref, own_w_ref, got_w_ref, *outs):
    own = own_ref[...].reshape(-1, PAIR)
    got = got_ref[...].reshape(-1, PAIR)
    step = 256
    for n in range(own_w_ref.shape[1] // step):
        lanes = pl.ds(n * step, step)
        result = jnp.dot(own, own_w_ref[:, lanes], preferred_element_type=jnp.float32)
        result = result + jnp.dot(got, got_w_ref[:, lanes], preferred_element_type=jnp.float32)
        result = result.astype(jnp.bfloat16).reshape(len(outs), SIDE, CORE_ROWS, step)
        for g, out in enumerate(outs):
            out[:, :, lanes] = result[g]


def project(part, own, got, own_w, got_w):
    width = got_w.shape[1] // PARTS
    rows = pl.BlockSpec((CHIPS, CORE_ROWS, PAIR), lambda i: (0, 0, 0))
    weight = pl.BlockSpec((PAIR, width), lambda i: (0, part), pipeline_mode=pl.Buffered(1))
    out = jax.ShapeDtypeStruct((SIDE, CORE_ROWS, width), jnp.bfloat16)
    return pl.pallas_call(
        project_kernel,
        out_shape=(out,) * SIDE,
        grid=(1,),
        in_specs=[rows, rows, weight, weight],
        out_specs=(pl.BlockSpec((SIDE, CORE_ROWS, width), lambda i: (0, 0, 0)),) * SIDE,
        compiler_params=pltpu.CompilerParams(vmem_limit_bytes=24 << 20),
    )(own, got, own_w, got_w)


def add_lines_kernel(*refs):
    ins, outs = refs[:SIDE], refs[SIDE:]
    for t, out in enumerate(outs):
        total = ins[0][t].astype(jnp.float32)
        for ref in ins[1:]:
            total = total + ref[t].astype(jnp.float32)
        out[...] = total.astype(jnp.bfloat16)


def add_lines(parts):
    width = parts[0].shape[2]
    return pl.pallas_call(
        add_lines_kernel,
        out_shape=(jax.ShapeDtypeStruct((CORE_ROWS, width), jnp.bfloat16),) * SIDE,
        in_specs=whole(SIDE),
        compiler_params=pltpu.CompilerParams(vmem_limit_bytes=8 << 20),
        name="add_lines",
    )(*parts)


def add_rows_kernel(*refs):
    out_ref = refs[-1]
    width = out_ref.shape[1] // PARTS
    for n in range(PARTS):
        lanes = pl.ds(n * width, width)
        ins = refs[n * SIDE:(n + 1) * SIDE]
        total = ins[0][...].astype(jnp.float32)
        for part in ins[1:]:
            total = total + part[...].astype(jnp.float32)
        out_ref[:, lanes] = total.astype(jnp.bfloat16)


def add_rows(parts):
    rows, width = parts[0].shape
    return pl.pallas_call(
        add_rows_kernel,
        out_shape=jax.ShapeDtypeStruct((rows, PARTS * width), jnp.bfloat16),
        in_specs=whole(len(parts)),
        compiler_params=pltpu.CompilerParams(vmem_limit_bytes=8 << 20),
        name="add_rows",
    )(*parts)


def step(queries, probes, keys, values, w_out):
    core = lax.axis_index("c")
    first = core == 0
    table = table_of(lax.axis_index("x"), lax.axis_index("z"), core)
    wide = lax.all_gather(w_out, "y", axis=1, tiled=True)

    own_query, send_query = split_query(table, queries)
    got_query = swap(send_query)
    chip_query = jnp.where(
        first,
        jnp.concatenate([own_query, got_query], 1),
        jnp.concatenate([got_query, own_query], 1),
    )
    lines = [chip_query]
    for s in (1, 2, 3):
        lines.append(send(chip_query, "b", s))

    send_keys, send_values = other_half(table, keys, values)
    other_keys, other_values = swap(send_keys), swap(send_values)

    where = {}
    spread = spread_query(table, lines)
    for g, ks in enumerate(GROUPS):
        sources = [spread[g * SIDE]]
        for s in SHIFTS:
            sources.append(send(spread[g * SIDE + s], "a", s))
        for i, k in enumerate(ks):
            where[k] = (i, sources)

    head_probes = jnp.transpose(probes, (1, 2, 0))
    parts = []
    for k, start, count in CALLS:
        place, sources = where[k]
        part = attend(
            table, k, start, count, place, sources, keys, other_keys, values, other_values, head_probes
        )
        if k < SIDE - 1:
            part = send(part, "a", k + 1)
        parts.append(part)
    wide, parts[-1] = lax.optimization_barrier((wide, parts[-1]))
    got_wide = swap(wide)
    merged = combine(parts)
    passed = [merged[0]]
    for t in (1, 2, 3):
        passed.append(send(merged[t], "b", t))
    own_rows, send_rows = finish(table, passed)
    got_rows = swap(send_rows)

    projected = [project(n, own_rows, got_rows, wide, got_wide) for n in range(PARTS)]
    gathered = []
    for groups in projected:
        arrived = [groups[3]]
        for s in SHIFTS:
            arrived.append(send(groups[s - 1], "a", s))
        gathered.append(arrived)
    last = []
    for arrived in gathered:
        summed = add_lines(arrived)
        last.append(summed[0])
        for t in SHIFTS:
            last.append(send(summed[t], "b", t))
    return add_rows(last)


def solution(mesh):
    fine = Mesh(mesh.devices.reshape(4, SIDE, SIDE, 2), ("y",) + MEM)
    placed = (
        P(("y",) + MEM, None),
        P("y", None, None),
        P("y", MEM, None),
        P("y", MEM, None),
        P(MEM, "y"),
    )
    return jax.shard_map(
        step, mesh=fine, in_specs=placed, out_specs=P(("y",) + MEM, None), check_vma=False
    )
```

```python
import functools

import jax
import jax.numpy as jnp
from jax import lax
from jax.experimental import pallas as pl
from jax.experimental.pallas import tpu as pltpu
from jax.sharding import Mesh
from jax.sharding import PartitionSpec as P


DH = 128
BLOCK = 256
PAIR = 2 * DH
SIDE = 4
CHIPS = SIDE * SIDE
ROWS = 512
KEYS = 512
CHIP_ROWS = ROWS // CHIPS
CORE_ROWS = CHIP_ROWS // 2
STAT = 16
UNIT = 256
CHUNK = 64
PARTS = 2
PART = PAIR + STAT
NEG = -1e30
SCALE = DH ** -0.5 * 1.4426950408889634

MEM = ("x", "z", "c")
GROUPS = ((0,), (1,), (2, 3))
CALLS = ((0, 0, 4), (1, 0, 4), (2, 0, 4), (3, 0, 4))
SHIFTS = (1, 2, 3)
SWAP = [(0, 1), (1, 0)]

CORE = 0
BLOCKS = 1
PAIRS = 5
OTHER_PAIRS = PAIRS + CHIPS
ROW_AT = OTHER_PAIRS + CHIPS
MY_A = ROW_AT + CHIPS
MY_B = MY_A + 1


def shift(axis, step):
    moves = []
    for x in range(SIDE):
        for z in range(SIDE):
            for c in range(2):
                along_z = (axis == "a") == (c == 0)
                to_x = x if along_z else (x + step) % SIDE
                to_z = (z + step) % SIDE if along_z else z
                moves.append(((x * SIDE + z) * 2 + c, (to_x * SIDE + to_z) * 2 + c))
    return moves


def send(value, axis, step):
    return lax.ppermute(value, MEM, shift(axis, step))


def swap(value):
    return lax.ppermute(value, "c", SWAP)


def table_of(x, z, core):
    a = jnp.where(core == 0, z, x)
    b = jnp.where(core == 0, x, z)
    major = jnp.arange(CHIPS, dtype=jnp.int32) // SIDE
    minor = jnp.arange(CHIPS, dtype=jnp.int32) % SIDE

    def chip_at(along_a, along_b, on_core):
        return jnp.where(on_core == 0, along_b * SIDE + along_a, along_a * SIDE + along_b)

    own_block = ((x * SIDE + z) * 2 + core) * 2
    other_block = ((x * SIDE + z) * 2 + 1 - core) * 2
    blocks = jnp.where(jnp.arange(4) < 2, own_block, other_block) + jnp.arange(4) % 2
    pairs = chip_at((a + 1 + major) % SIDE, (b + minor) % SIDE, core)
    other_pairs = chip_at((b + 1 + major) % SIDE, (a + minor) % SIDE, 1 - core)
    row_at = chip_at((a + SIDE - major) % SIDE, minor, core) * CHIP_ROWS
    parts = [core.reshape(1), blocks, pairs, other_pairs, row_at, a.reshape(1), b.reshape(1)]
    return jnp.concatenate([p.astype(jnp.int32) for p in parts])


def whole(count):
    return [pl.BlockSpec(memory_space=pltpu.VMEM)] * count


def split_query_kernel(table, q_ref, own_ref, other_ref):
    first = table[CORE] == 0
    for p in range(CHIPS):
        turned = (p % SIDE) * SIDE + p // SIDE
        zero = q_ref[:, 2 * turned * PAIR:(2 * turned + 1) * PAIR]
        one = q_ref[:, (2 * p + 1) * PAIR:(2 * p + 2) * PAIR]
        here = pl.ds((p % SIDE) * PAIR, PAIR)
        own_ref[p // SIDE, :, here] = jnp.where(first, zero, one)
        other_ref[p // SIDE, :, here] = jnp.where(first, one, zero)


def split_query(table, queries):
    rows = queries.shape[0]
    half = jax.ShapeDtypeStruct((SIDE, rows, SIDE * PAIR), queries.dtype)
    return pl.pallas_call(
        split_query_kernel,
        out_shape=(half, half),
        in_specs=[pl.BlockSpec(memory_space=pltpu.SMEM)] + whole(1),
        compiler_params=pltpu.CompilerParams(vmem_limit_bytes=8 << 20),
        name="split_query",
    )(table, queries)


def spread_query_kernel(table, *refs):
    lines, outs = refs[:SIDE], refs[SIDE:]
    a, b = table[MY_A], table[MY_B]
    for t in range(SIDE):
        at = pl.ds(pl.multiple_of(((b + SIDE - t) % SIDE) * CHIP_ROWS, CHIP_ROWS), CHIP_ROWS)
        for g, ks in enumerate(GROUPS):
            for s in range(SIDE):
                for i, k in enumerate(ks):
                    group = (a + s + 1 + k) % SIDE
                    outs[g * SIDE + s][i, at, :] = lines[t][group]


def spread_query(table, lines):
    pieces = [
        jax.ShapeDtypeStruct((len(ks), SIDE * CHIP_ROWS, SIDE * PAIR), lines[0].dtype)
        for ks in GROUPS
        for _ in range(SIDE)
    ]
    return pl.pallas_call(
        spread_query_kernel,
        out_shape=tuple(pieces),
        in_specs=[pl.BlockSpec(memory_space=pltpu.SMEM)] + whole(SIDE),
        compiler_params=pltpu.CompilerParams(vmem_limit_bytes=16 << 20),
        name="spread_query",
    )(table, *lines)


def other_half_kernel(table, *refs):
    del table
    ins, outs = refs[:2 * SIDE], refs[2 * SIDE:]
    for n, out in enumerate(outs):
        for j in range(SIDE):
            out[:, j * PAIR:(j + 1) * PAIR] = ins[n * SIDE + j][0]


def other_half(table, keys, values):
    half = jax.ShapeDtypeStruct((KEYS, CHIPS * PAIR), keys.dtype)

    def source(j):
        return pl.BlockSpec(
            (1, KEYS, PAIR), lambda i, table: (0, 0, 2 * (i * SIDE + j) + 1 - table[CORE])
        )

    return pl.pallas_call(
        other_half_kernel,
        out_shape=(half, half),
        grid_spec=pltpu.PrefetchScalarGridSpec(
            num_scalar_prefetch=1,
            grid=(SIDE,),
            in_specs=[source(j) for j in range(SIDE)] * 2,
            out_specs=(pl.BlockSpec((KEYS, SIDE * PAIR), lambda i, table: (0, i)),) * 2,
        ),
        name="other_half",
    )(table, *[keys] * SIDE, *[values] * SIDE)


def attend_kernel(
    table, q0, q1, q2, q3, ka_ref, kb_ref, va_ref, vb_ref, probe_ref, out_ref,
    q_ref, s_ref, p_ref, v_ref, *, call, place,
):
    pair = table[PAIRS + call + pl.program_id(0)]
    turn = (table[MY_B] + call + pl.program_id(0)) % SIDE
    columns = pl.ds(pl.multiple_of(turn * PAIR, PAIR), PAIR)
    for s, source in enumerate((q0, q1, q2, q3)):
        for b in range(SIDE):
            at = pl.multiple_of(table[ROW_AT + s * SIDE + b], CHIP_ROWS)
            q_ref[pl.ds(at, CHIP_ROWS), :] = source[place, b * CHIP_ROWS:(b + 1) * CHIP_ROWS, columns]
    probe_at = 2 * pair + table[CORE]

    def other_lanes(h):
        return pl.ds(pl.multiple_of(pair * PAIR + h * DH, DH), DH)

    v_ref[:, :, DH:, :] = jnp.ones((2, 2, STAT, KEYS), jnp.bfloat16)

    units = [(h, r) for h in range(2) for r in range(ROWS // UNIT)]
    stat_row = lax.broadcasted_iota(jnp.int32, (STAT, UNIT), 0)
    stats = [jnp.zeros((STAT, UNIT), jnp.float32) for _ in range(ROWS // UNIT)]

    def block_tops(u, b):
        h, r = units[u]
        lanes = pl.ds(h * DH, DH)
        span = pl.ds((b % 2) * BLOCK, BLOCK)
        key = ka_ref[0, span, lanes] if b < 2 else kb_ref[span, other_lanes(h)]
        score = lax.dot_general(
            key, q_ref[r * UNIT:(r + 1) * UNIT, lanes], (((1,), (1,)), ((), ())),
            preferred_element_type=jnp.float32,
        )
        s_ref[u % 2, b] = score
        return jnp.max(score.reshape(-1, 8, UNIT), axis=0)

    def offsets(u, tops):
        h, r = units[u]
        probe = probe_ref[2 * probe_at + h, :, r * UNIT:(r + 1) * UNIT]
        top = jnp.full((1, UNIT), NEG, jnp.float32)
        hits = []
        for b in range(4):
            hit = jnp.max(jnp.where(probe == table[BLOCKS + b], 1.0, 0.0), axis=0, keepdims=True) > 0.5
            top = jnp.maximum(top, jnp.where(hit, jnp.max(tops[b], axis=0, keepdims=True), NEG))
            hits.append(hit)
        top = (top * SCALE).astype(jnp.bfloat16).astype(jnp.float32)
        return top, [jnp.where(hit, top, -NEG) for hit in hits]

    tops = [block_tops(0, b) for b in range(4)]
    for u, (h, r) in enumerate(units):
        top, offset = offsets(u, tops)
        tops = []
        lanes = pl.ds(h * DH, DH)
        if r == 0:
            v_ref[h, 0, :DH, :] = jnp.transpose(va_ref[0, :, lanes])
            v_ref[h, 1, :DH, :] = jnp.transpose(vb_ref[:, other_lanes(h)])
        for b in range(4):
            if u + 1 < len(units):
                tops.append(block_tops(u + 1, b))
            for c in range(0, BLOCK, CHUNK):
                weight = jnp.exp2(s_ref[u % 2, b, c:c + CHUNK, :] * SCALE - offset[b])
                p_ref[u % 2, b * BLOCK + c:b * BLOCK + c + CHUNK, :] = weight.astype(jnp.bfloat16)
        sums = jnp.dot(
            v_ref[h, 0], p_ref[u % 2, :KEYS, :], preferred_element_type=jnp.float32
        ) + jnp.dot(v_ref[h, 1], p_ref[u % 2, KEYS:, :], preferred_element_type=jnp.float32)
        out_ref[0, h * DH:(h + 1) * DH, r * UNIT:(r + 1) * UNIT] = sums[:DH].astype(jnp.bfloat16)
        total = sums[DH:DH + 1]
        high = total.astype(jnp.bfloat16).astype(jnp.float32)
        for j, row in enumerate((top, high, total - high)):
            stats[r] = jnp.where(stat_row == 3 * h + j, row, stats[r])
    for r, rows in enumerate(stats):
        out_ref[0, PAIR:, r * UNIT:(r + 1) * UNIT] = rows.astype(jnp.bfloat16)


def attend(table, k, start, count, place, sources, keys, other_keys, values, other_values, probes):
    own = pl.BlockSpec(
        (1, KEYS, PAIR),
        lambda j, table: (0, 0, 2 * table[PAIRS + k * SIDE + start + j] + table[CORE]),
    )
    here = pl.BlockSpec(memory_space=pltpu.VMEM)
    return pl.pallas_call(
        functools.partial(attend_kernel, call=k * SIDE + start, place=place),
        out_shape=jax.ShapeDtypeStruct((count, PART, ROWS), jnp.bfloat16),
        grid_spec=pltpu.PrefetchScalarGridSpec(
            num_scalar_prefetch=1,
            grid=(count,),
            in_specs=[here] * SIDE + [own, here, own, here, here],
            out_specs=pl.BlockSpec((1, PART, ROWS), lambda j, table: (j, 0, 0)),
            scratch_shapes=[
                pltpu.VMEM((ROWS, PAIR), jnp.bfloat16),
                pltpu.VMEM((2, 4, BLOCK, UNIT), jnp.float32),
                pltpu.VMEM((2, 2 * KEYS, UNIT), jnp.bfloat16),
                pltpu.VMEM((2, 2, DH + STAT, KEYS), jnp.bfloat16),
            ],
        ),
        compiler_params=pltpu.CompilerParams(vmem_limit_bytes=40 << 20),
    )(table, *sources, keys, other_keys, values, other_values, probes)


def merge(parts, h):
    tops = [part[PAIR + 3 * h:PAIR + 3 * h + 1, :].astype(jnp.float32) for part in parts]
    top = tops[0]
    for other in tops[1:]:
        top = jnp.maximum(top, other)
    total = jnp.zeros_like(top)
    numerator = jnp.zeros((DH, top.shape[1]), jnp.float32)
    for part, part_top in zip(parts, tops):
        scale = jnp.exp2(part_top - top)
        high = part[PAIR + 3 * h + 1:PAIR + 3 * h + 2, :].astype(jnp.float32)
        low = part[PAIR + 3 * h + 2:PAIR + 3 * h + 3, :].astype(jnp.float32)
        total = total + scale * (high + low)
        numerator = numerator + scale * part[h * DH:(h + 1) * DH, :].astype(jnp.float32)
    return top, total, numerator


def stat_rows(stats, h, top, total):
    stat_row = lax.broadcasted_iota(jnp.int32, stats.shape, 0)
    high = total.astype(jnp.bfloat16).astype(jnp.float32)
    for j, row in enumerate((top, high, total - high)):
        stats = jnp.where(stat_row == 3 * h + j, row, stats)
    return stats


def combine_kernel(*refs):
    ins, outs = refs[:-SIDE], refs[-SIDE:]
    lines = [[] for _ in range(SIDE)]
    at = 0
    for ref in ins:
        for i in range(ref.shape[0]):
            lines[at % SIDE].append(ref.at[i])
            at += 1
    for parts, out in zip(lines, outs):
        stats = jnp.zeros((STAT, ROWS), jnp.float32)
        for h in range(2):
            top, total, numerator = merge(parts, h)
            out[h * DH:(h + 1) * DH, :] = numerator.astype(jnp.bfloat16)
            stats = stat_rows(stats, h, top, total)
        out[PAIR:, :] = stats.astype(jnp.bfloat16)


def combine(parts):
    return pl.pallas_call(
        combine_kernel,
        out_shape=(jax.ShapeDtypeStruct((PART, ROWS), jnp.bfloat16),) * SIDE,
        in_specs=whole(len(parts)),
        compiler_params=pltpu.CompilerParams(vmem_limit_bytes=16 << 20),
        name="combine",
    )(*parts)


def finish_kernel(table, *refs):
    ins, own_ref, other_ref, rows_ref = refs[:SIDE], refs[SIDE], refs[SIDE + 1], refs[SIDE + 2]
    for h in range(2):
        _, total, numerator = merge(ins, h)
        rows_ref[:, h * DH:(h + 1) * DH] = jnp.transpose(numerator / total).astype(jnp.bfloat16)
    for ref, at, core in ((own_ref, PAIRS, table[CORE]), (other_ref, OTHER_PAIRS, 1 - table[CORE])):
        for p in range(CHIPS):
            start = pl.multiple_of(table[at + p] * CHIP_ROWS + core * CORE_ROWS, CORE_ROWS)
            ref[p] = rows_ref[pl.ds(start, CORE_ROWS), :]


def finish(table, parts):
    rows = jax.ShapeDtypeStruct((CHIPS, CORE_ROWS, PAIR), jnp.bfloat16)
    return pl.pallas_call(
        finish_kernel,
        out_shape=(rows, rows),
        in_specs=[pl.BlockSpec(memory_space=pltpu.SMEM)] + whole(SIDE),
        scratch_shapes=[pltpu.VMEM((ROWS, PAIR), jnp.bfloat16)],
        compiler_params=pltpu.CompilerParams(vmem_limit_bytes=12 << 20),
        name="finish",
    )(table, *parts)


def project_kernel(own_ref, got_ref, own_w_ref, got_w_ref, *outs):
    own = own_ref[...].reshape(-1, PAIR)
    got = got_ref[...].reshape(-1, PAIR)
    step = 256
    for n in range(own_w_ref.shape[1] // step):
        lanes = pl.ds(n * step, step)
        result = jnp.dot(own, own_w_ref[:, lanes], preferred_element_type=jnp.float32)
        result = result + jnp.dot(got, got_w_ref[:, lanes], preferred_element_type=jnp.float32)
        result = result.astype(jnp.bfloat16).reshape(len(outs), SIDE, CORE_ROWS, step)
        for g, out in enumerate(outs):
            out[:, :, lanes] = result[g]


def project(part, own, got, own_w, got_w):
    width = got_w.shape[1] // PARTS
    rows = pl.BlockSpec((CHIPS, CORE_ROWS, PAIR), lambda i: (0, 0, 0))
    weight = pl.BlockSpec((PAIR, width), lambda i: (0, part), pipeline_mode=pl.Buffered(1))
    out = jax.ShapeDtypeStruct((SIDE, CORE_ROWS, width), jnp.bfloat16)
    return pl.pallas_call(
        project_kernel,
        out_shape=(out,) * SIDE,
        grid=(1,),
        in_specs=[rows, rows, weight, weight],
        out_specs=(pl.BlockSpec((SIDE, CORE_ROWS, width), lambda i: (0, 0, 0)),) * SIDE,
        compiler_params=pltpu.CompilerParams(vmem_limit_bytes=24 << 20),
    )(own, got, own_w, got_w)


def add_lines_kernel(*refs):
    ins, outs = refs[:SIDE], refs[SIDE:]
    for t, out in enumerate(outs):
        total = ins[0][t].astype(jnp.float32)
        for ref in ins[1:]:
            total = total + ref[t].astype(jnp.float32)
        out[...] = total.astype(jnp.bfloat16)


def add_lines(parts):
    width = parts[0].shape[2]
    return pl.pallas_call(
        add_lines_kernel,
        out_shape=(jax.ShapeDtypeStruct((CORE_ROWS, width), jnp.bfloat16),) * SIDE,
        in_specs=whole(SIDE),
        compiler_params=pltpu.CompilerParams(vmem_limit_bytes=8 << 20),
        name="add_lines",
    )(*parts)


def add_rows_kernel(*refs):
    out_ref = refs[-1]
    width = out_ref.shape[1] // PARTS
    for n in range(PARTS):
        lanes = pl.ds(n * width, width)
        ins = refs[n * SIDE:(n + 1) * SIDE]
        total = ins[0][...].astype(jnp.float32)
        for part in ins[1:]:
            total = total + part[...].astype(jnp.float32)
        out_ref[:, lanes] = total.astype(jnp.bfloat16)


def add_rows(parts):
    rows, width = parts[0].shape
    return pl.pallas_call(
        add_rows_kernel,
        out_shape=jax.ShapeDtypeStruct((rows, PARTS * width), jnp.bfloat16),
        in_specs=whole(len(parts)),
        compiler_params=pltpu.CompilerParams(vmem_limit_bytes=8 << 20),
        name="add_rows",
    )(*parts)


def step(queries, probes, keys, values, w_out):
    core = lax.axis_index("c")
    first = core == 0
    table = table_of(lax.axis_index("x"), lax.axis_index("z"), core)
    wide = lax.all_gather(w_out, "y", axis=1, tiled=True)

    own_query, send_query = split_query(table, queries)
    got_query = swap(send_query)
    chip_query = jnp.where(
        first,
        jnp.concatenate([own_query, got_query], 1),
        jnp.concatenate([got_query, own_query], 1),
    )
    lines = [chip_query]
    for s in (1, 2, 3):
        lines.append(send(chip_query, "b", s))

    send_keys, send_values = other_half(table, keys, values)
    other_keys, other_values = swap(send_keys), swap(send_values)

    where = {}
    spread = spread_query(table, lines)
    for g, ks in enumerate(GROUPS):
        sources = [spread[g * SIDE]]
        for s in SHIFTS:
            sources.append(send(spread[g * SIDE + s], "a", s))
        for i, k in enumerate(ks):
            where[k] = (i, sources)

    head_probes = jnp.transpose(probes, (1, 2, 0))
    parts = []
    for k, start, count in CALLS:
        place, sources = where[k]
        part = attend(
            table, k, start, count, place, sources, keys, other_keys, values, other_values, head_probes
        )
        if k < SIDE - 1:
            part = send(part, "a", k + 1)
        parts.append(part)
    wide, parts[-1] = lax.optimization_barrier((wide, parts[-1]))
    got_wide = swap(wide)
    merged = combine(parts)
    passed = [merged[0]]
    for t in (1, 2, 3):
        passed.append(send(merged[t], "b", t))
    own_rows, send_rows = finish(table, passed)
    got_rows = swap(send_rows)

    projected = [project(n, own_rows, got_rows, wide, got_wide) for n in range(PARTS)]
    gathered = []
    for groups in projected:
        arrived = [groups[3]]
        for s in SHIFTS:
            arrived.append(send(groups[s - 1], "a", s))
        gathered.append(arrived)
    last = []
    for arrived in gathered:
        summed = add_lines(arrived)
        last.append(summed[0])
        for t in SHIFTS:
            last.append(send(summed[t], "b", t))
    return add_rows(last)


def solution(mesh):
    fine = Mesh(mesh.devices.reshape(4, SIDE, SIDE, 2), ("y",) + MEM)
    placed = (
        P(("y",) + MEM, None),
        P("y", None, None),
        P("y", MEM, None),
        P("y", MEM, None),
        P(MEM, "y"),
    )
    return jax.shard_map(
        step, mesh=fine, in_specs=placed, out_specs=P(("y",) + MEM, None), check_vma=False
    )
```

```python
import functools

import jax
import jax.numpy as jnp
from jax import lax
from jax.experimental import pallas as pl
from jax.experimental.pallas import tpu as pltpu
from jax.sharding import Mesh
from jax.sharding import PartitionSpec as P


DH = 128
BLOCK = 256
PAIR = 2 * DH
SIDE = 4
CHIPS = SIDE * SIDE
ROWS = 512
KEYS = 512
CHIP_ROWS = ROWS // CHIPS
CORE_ROWS = CHIP_ROWS // 2
STAT = 16
UNIT = 256
CHUNK = 64
PARTS = 2
PART = PAIR + STAT
NEG = -1e30
SCALE = DH ** -0.5 * 1.4426950408889634

MEM = ("x", "z", "c")
GROUPS = ((0,), (1, 2), (3,))
CALLS = ((0, (4,)), (4, (4, 2)), (10, (2,)), (12, (4,)))
SHIFTS = (1, 2, 3)
SWAP = [(0, 1), (1, 0)]

CORE = 0
BLOCKS = 1
PAIRS = 5
OTHER_PAIRS = PAIRS + CHIPS
ROW_AT = OTHER_PAIRS + CHIPS
MY_A = ROW_AT + CHIPS
MY_B = MY_A + 1


def shift(axis, step):
    moves = []
    for x in range(SIDE):
        for z in range(SIDE):
            for c in range(2):
                along_z = (axis == "a") == (c == 0)
                to_x = x if along_z else (x + step) % SIDE
                to_z = (z + step) % SIDE if along_z else z
                moves.append(((x * SIDE + z) * 2 + c, (to_x * SIDE + to_z) * 2 + c))
    return moves


def send(value, axis, step):
    return lax.ppermute(value, MEM, shift(axis, step))


def swap(value):
    return lax.ppermute(value, "c", SWAP)


def table_of(x, z, core):
    a = jnp.where(core == 0, z, x)
    b = jnp.where(core == 0, x, z)
    major = jnp.arange(CHIPS, dtype=jnp.int32) // SIDE
    minor = jnp.arange(CHIPS, dtype=jnp.int32) % SIDE

    def chip_at(along_a, along_b, on_core):
        return jnp.where(on_core == 0, along_b * SIDE + along_a, along_a * SIDE + along_b)

    own_block = ((x * SIDE + z) * 2 + core) * 2
    other_block = ((x * SIDE + z) * 2 + 1 - core) * 2
    blocks = jnp.where(jnp.arange(4) < 2, own_block, other_block) + jnp.arange(4) % 2
    pairs = chip_at((a + 1 + major) % SIDE, (b + minor) % SIDE, core)
    other_pairs = chip_at((b + 1 + major) % SIDE, (a + minor) % SIDE, 1 - core)
    row_at = chip_at((a + SIDE - major) % SIDE, minor, core) * CHIP_ROWS
    parts = [core.reshape(1), blocks, pairs, other_pairs, row_at, a.reshape(1), b.reshape(1)]
    return jnp.concatenate([p.astype(jnp.int32) for p in parts])


def whole(count):
    return [pl.BlockSpec(memory_space=pltpu.VMEM)] * count


def split_query_kernel(table, q_ref, own_ref, other_ref):
    first = table[CORE] == 0
    for p in range(CHIPS):
        turned = (p % SIDE) * SIDE + p // SIDE
        zero = q_ref[:, 2 * turned * PAIR:(2 * turned + 1) * PAIR]
        one = q_ref[:, (2 * p + 1) * PAIR:(2 * p + 2) * PAIR]
        here = pl.ds((p % SIDE) * PAIR, PAIR)
        own_ref[p // SIDE, :, here] = jnp.where(first, zero, one)
        other_ref[p // SIDE, :, here] = jnp.where(first, one, zero)


def split_query(table, queries):
    rows = queries.shape[0]
    half = jax.ShapeDtypeStruct((SIDE, rows, SIDE * PAIR), queries.dtype)
    return pl.pallas_call(
        split_query_kernel,
        out_shape=(half, half),
        in_specs=[pl.BlockSpec(memory_space=pltpu.SMEM)] + whole(1),
        compiler_params=pltpu.CompilerParams(vmem_limit_bytes=8 << 20),
        name="split_query",
    )(table, queries)


def spread_query_kernel(table, *refs):
    lines, outs = refs[:SIDE], refs[SIDE:]
    a, b = table[MY_A], table[MY_B]
    for t in range(SIDE):
        at = pl.ds(pl.multiple_of(((b + SIDE - t) % SIDE) * CHIP_ROWS, CHIP_ROWS), CHIP_ROWS)
        for g, ks in enumerate(GROUPS):
            for s in range(SIDE):
                for i, k in enumerate(ks):
                    group = (a + s + 1 + k) % SIDE
                    outs[g * SIDE + s][i, at, :] = lines[t][group]


def spread_query(table, lines):
    pieces = [
        jax.ShapeDtypeStruct((len(ks), SIDE * CHIP_ROWS, SIDE * PAIR), lines[0].dtype)
        for ks in GROUPS
        for _ in range(SIDE)
    ]
    return pl.pallas_call(
        spread_query_kernel,
        out_shape=tuple(pieces),
        in_specs=[pl.BlockSpec(memory_space=pltpu.SMEM)] + whole(SIDE),
        compiler_params=pltpu.CompilerParams(vmem_limit_bytes=16 << 20),
        name="spread_query",
    )(table, *lines)


def other_half_kernel(table, *refs):
    del table
    ins, outs = refs[:2 * SIDE], refs[2 * SIDE:]
    for n, out in enumerate(outs):
        for j in range(SIDE):
            out[:, j * PAIR:(j + 1) * PAIR] = ins[n * SIDE + j][0]


def other_half(table, keys, values):
    half = jax.ShapeDtypeStruct((KEYS, CHIPS * PAIR), keys.dtype)

    def source(j):
        return pl.BlockSpec(
            (1, KEYS, PAIR), lambda i, table: (0, 0, 2 * (i * SIDE + j) + 1 - table[CORE])
        )

    return pl.pallas_call(
        other_half_kernel,
        out_shape=(half, half),
        grid_spec=pltpu.PrefetchScalarGridSpec(
            num_scalar_prefetch=1,
            grid=(SIDE,),
            in_specs=[source(j) for j in range(SIDE)] * 2,
            out_specs=(pl.BlockSpec((KEYS, SIDE * PAIR), lambda i, table: (0, i)),) * 2,
        ),
        name="other_half",
    )(table, *[keys] * SIDE, *[values] * SIDE)


def attend_kernel(
    table, q0, q1, q2, q3, ka_ref, kb_ref, va_ref, vb_ref, probe_ref, *refs, call, group, sizes
):
    outs = refs[:len(sizes)]
    q_ref, s_ref, p_ref, v_ref, o_ref = refs[len(sizes):]
    place = (call + pl.program_id(0)) // SIDE - group
    out_ref = o_ref if len(sizes) > 1 else outs[0]
    pair = table[PAIRS + call + pl.program_id(0)]
    turn = (table[MY_B] + call + pl.program_id(0)) % SIDE
    columns = pl.ds(pl.multiple_of(turn * PAIR, PAIR), PAIR)
    for s, source in enumerate((q0, q1, q2, q3)):
        for b in range(SIDE):
            at = pl.multiple_of(table[ROW_AT + s * SIDE + b], CHIP_ROWS)
            q_ref[pl.ds(at, CHIP_ROWS), :] = source[place, b * CHIP_ROWS:(b + 1) * CHIP_ROWS, columns]
    probe_at = 2 * pair + table[CORE]

    def other_lanes(h):
        return pl.ds(pl.multiple_of(pair * PAIR + h * DH, DH), DH)

    v_ref[:, :, DH:, :] = jnp.ones((2, 2, STAT, KEYS), jnp.bfloat16)

    units = [(h, r) for h in range(2) for r in range(ROWS // UNIT)]
    stat_row = lax.broadcasted_iota(jnp.int32, (STAT, UNIT), 0)
    stats = [jnp.zeros((STAT, UNIT), jnp.float32) for _ in range(ROWS // UNIT)]

    def block_tops(u, b):
        h, r = units[u]
        lanes = pl.ds(h * DH, DH)
        span = pl.ds((b % 2) * BLOCK, BLOCK)
        key = ka_ref[0, span, lanes] if b < 2 else kb_ref[span, other_lanes(h)]
        score = lax.dot_general(
            key, q_ref[r * UNIT:(r + 1) * UNIT, lanes], (((1,), (1,)), ((), ())),
            preferred_element_type=jnp.float32,
        )
        s_ref[u % 2, b] = score
        return jnp.max(score.reshape(-1, 8, UNIT), axis=0)

    def offsets(u, tops):
        h, r = units[u]
        probe = probe_ref[2 * probe_at + h, :, r * UNIT:(r + 1) * UNIT]
        top = jnp.full((1, UNIT), NEG, jnp.float32)
        hits = []
        for b in range(4):
            hit = jnp.max(jnp.where(probe == table[BLOCKS + b], 1.0, 0.0), axis=0, keepdims=True) > 0.5
            top = jnp.maximum(top, jnp.where(hit, jnp.max(tops[b], axis=0, keepdims=True), NEG))
            hits.append(hit)
        top = (top * SCALE).astype(jnp.bfloat16).astype(jnp.float32)
        return top, [jnp.where(hit, top, -NEG) for hit in hits]

    tops = [block_tops(0, b) for b in range(4)]
    for u, (h, r) in enumerate(units):
        top, offset = offsets(u, tops)
        tops = []
        lanes = pl.ds(h * DH, DH)
        if r == 0:
            v_ref[h, 0, :DH, :] = jnp.transpose(va_ref[0, :, lanes])
            v_ref[h, 1, :DH, :] = jnp.transpose(vb_ref[:, other_lanes(h)])
        for b in range(4):
            if u + 1 < len(units):
                tops.append(block_tops(u + 1, b))
            for c in range(0, BLOCK, CHUNK):
                weight = jnp.exp2(s_ref[u % 2, b, c:c + CHUNK, :] * SCALE - offset[b])
                p_ref[u % 2, b * BLOCK + c:b * BLOCK + c + CHUNK, :] = weight.astype(jnp.bfloat16)
        sums = jnp.dot(
            v_ref[h, 0], p_ref[u % 2, :KEYS, :], preferred_element_type=jnp.float32
        ) + jnp.dot(v_ref[h, 1], p_ref[u % 2, KEYS:, :], preferred_element_type=jnp.float32)
        out_ref[0, h * DH:(h + 1) * DH, r * UNIT:(r + 1) * UNIT] = sums[:DH].astype(jnp.bfloat16)
        total = sums[DH:DH + 1]
        high = total.astype(jnp.bfloat16).astype(jnp.float32)
        for j, row in enumerate((top, high, total - high)):
            stats[r] = jnp.where(stat_row == 3 * h + j, row, stats[r])
    for r, rows in enumerate(stats):
        out_ref[0, PAIR:, r * UNIT:(r + 1) * UNIT] = rows.astype(jnp.bfloat16)
    if len(sizes) > 1:
        step = pl.program_id(0)

        @pl.when(step < sizes[0])
        def _():
            outs[0][...] = o_ref[...]

        @pl.when(step >= sizes[0])
        def _():
            outs[1][...] = o_ref[...]


def attend(table, call, sizes, group, sources, keys, other_keys, values, other_values, probes):
    own = pl.BlockSpec(
        (1, KEYS, PAIR), lambda j, table: (0, 0, 2 * table[PAIRS + call + j] + table[CORE])
    )
    here = pl.BlockSpec(memory_space=pltpu.VMEM)
    spots = [lambda j, table: (jnp.minimum(j, sizes[0] - 1), 0, 0)]
    if len(sizes) > 1:
        spots.append(lambda j, table: (jnp.maximum(j - sizes[0], 0), 0, 0))
    return pl.pallas_call(
        functools.partial(attend_kernel, call=call, group=group, sizes=sizes),
        out_shape=tuple(jax.ShapeDtypeStruct((n, PART, ROWS), jnp.bfloat16) for n in sizes),
        grid_spec=pltpu.PrefetchScalarGridSpec(
            num_scalar_prefetch=1,
            grid=(sum(sizes),),
            in_specs=[here] * SIDE + [own, here, own, here, here],
            out_specs=tuple(pl.BlockSpec((1, PART, ROWS), spot) for spot in spots),
            scratch_shapes=[
                pltpu.VMEM((ROWS, PAIR), jnp.bfloat16),
                pltpu.VMEM((2, 4, BLOCK, UNIT), jnp.float32),
                pltpu.VMEM((2, 2 * KEYS, UNIT), jnp.bfloat16),
                pltpu.VMEM((2, 2, DH + STAT, KEYS), jnp.bfloat16),
                pltpu.VMEM((1, PART, ROWS), jnp.bfloat16),
            ],
        ),
        compiler_params=pltpu.CompilerParams(vmem_limit_bytes=40 << 20),
    )(table, *sources, keys, other_keys, values, other_values, probes)


def merge(parts, h):
    tops = [part[PAIR + 3 * h:PAIR + 3 * h + 1, :].astype(jnp.float32) for part in parts]
    top = tops[0]
    for other in tops[1:]:
        top = jnp.maximum(top, other)
    total = jnp.zeros_like(top)
    numerator = jnp.zeros((DH, top.shape[1]), jnp.float32)
    for part, part_top in zip(parts, tops):
        scale = jnp.exp2(part_top - top)
        high = part[PAIR + 3 * h + 1:PAIR + 3 * h + 2, :].astype(jnp.float32)
        low = part[PAIR + 3 * h + 2:PAIR + 3 * h + 3, :].astype(jnp.float32)
        total = total + scale * (high + low)
        numerator = numerator + scale * part[h * DH:(h + 1) * DH, :].astype(jnp.float32)
    return top, total, numerator


def stat_rows(stats, h, top, total):
    stat_row = lax.broadcasted_iota(jnp.int32, stats.shape, 0)
    high = total.astype(jnp.bfloat16).astype(jnp.float32)
    for j, row in enumerate((top, high, total - high)):
        stats = jnp.where(stat_row == 3 * h + j, row, stats)
    return stats


def combine_kernel(*refs):
    ins, outs = refs[:-SIDE], refs[-SIDE:]
    lines = [[] for _ in range(SIDE)]
    at = 0
    for ref in ins:
        for i in range(ref.shape[0]):
            lines[at % SIDE].append(ref.at[i])
            at += 1
    for parts, out in zip(lines, outs):
        stats = jnp.zeros((STAT, ROWS), jnp.float32)
        for h in range(2):
            top, total, numerator = merge(parts, h)
            out[h * DH:(h + 1) * DH, :] = numerator.astype(jnp.bfloat16)
            stats = stat_rows(stats, h, top, total)
        out[PAIR:, :] = stats.astype(jnp.bfloat16)


def combine(parts):
    return pl.pallas_call(
        combine_kernel,
        out_shape=(jax.ShapeDtypeStruct((PART, ROWS), jnp.bfloat16),) * SIDE,
        in_specs=whole(len(parts)),
        compiler_params=pltpu.CompilerParams(vmem_limit_bytes=16 << 20),
        name="combine",
    )(*parts)


def finish_kernel(table, *refs):
    ins, own_ref, other_ref, rows_ref = refs[:SIDE], refs[SIDE], refs[SIDE + 1], refs[SIDE + 2]
    for h in range(2):
        _, total, numerator = merge(ins, h)
        rows_ref[:, h * DH:(h + 1) * DH] = jnp.transpose(numerator / total).astype(jnp.bfloat16)
    for ref, at, core in ((own_ref, PAIRS, table[CORE]), (other_ref, OTHER_PAIRS, 1 - table[CORE])):
        for p in range(CHIPS):
            start = pl.multiple_of(table[at + p] * CHIP_ROWS + core * CORE_ROWS, CORE_ROWS)
            ref[p] = rows_ref[pl.ds(start, CORE_ROWS), :]


def finish(table, parts):
    rows = jax.ShapeDtypeStruct((CHIPS, CORE_ROWS, PAIR), jnp.bfloat16)
    return pl.pallas_call(
        finish_kernel,
        out_shape=(rows, rows),
        in_specs=[pl.BlockSpec(memory_space=pltpu.SMEM)] + whole(SIDE),
        scratch_shapes=[pltpu.VMEM((ROWS, PAIR), jnp.bfloat16)],
        compiler_params=pltpu.CompilerParams(vmem_limit_bytes=12 << 20),
        name="finish",
    )(table, *parts)


def project_kernel(own_ref, got_ref, own_w_ref, got_w_ref, *outs):
    own = own_ref[...].reshape(-1, PAIR)
    got = got_ref[...].reshape(-1, PAIR)
    step = 256
    for n in range(own_w_ref.shape[1] // step):
        lanes = pl.ds(n * step, step)
        result = jnp.dot(own, own_w_ref[:, lanes], preferred_element_type=jnp.float32)
        result = result + jnp.dot(got, got_w_ref[:, lanes], preferred_element_type=jnp.float32)
        result = result.astype(jnp.bfloat16).reshape(len(outs), SIDE, CORE_ROWS, step)
        for g, out in enumerate(outs):
            out[:, :, lanes] = result[g]


def project(part, own, got, own_w, got_w):
    width = got_w.shape[1] // PARTS
    rows = pl.BlockSpec((CHIPS, CORE_ROWS, PAIR), lambda i: (0, 0, 0))
    weight = pl.BlockSpec((PAIR, width), lambda i: (0, part), pipeline_mode=pl.Buffered(1))
    out = jax.ShapeDtypeStruct((SIDE, CORE_ROWS, width), jnp.bfloat16)
    return pl.pallas_call(
        project_kernel,
        out_shape=(out,) * SIDE,
        grid=(1,),
        in_specs=[rows, rows, weight, weight],
        out_specs=(pl.BlockSpec((SIDE, CORE_ROWS, width), lambda i: (0, 0, 0)),) * SIDE,
        compiler_params=pltpu.CompilerParams(vmem_limit_bytes=24 << 20),
    )(own, got, own_w, got_w)


def add_lines_kernel(*refs):
    ins, outs = refs[:SIDE], refs[SIDE:]
    for t, out in enumerate(outs):
        total = ins[0][t].astype(jnp.float32)
        for ref in ins[1:]:
            total = total + ref[t].astype(jnp.float32)
        out[...] = total.astype(jnp.bfloat16)


def add_lines(parts):
    width = parts[0].shape[2]
    return pl.pallas_call(
        add_lines_kernel,
        out_shape=(jax.ShapeDtypeStruct((CORE_ROWS, width), jnp.bfloat16),) * SIDE,
        in_specs=whole(SIDE),
        compiler_params=pltpu.CompilerParams(vmem_limit_bytes=8 << 20),
        name="add_lines",
    )(*parts)


def add_rows_kernel(*refs):
    out_ref = refs[-1]
    width = out_ref.shape[1] // PARTS
    for n in range(PARTS):
        lanes = pl.ds(n * width, width)
        ins = refs[n * SIDE:(n + 1) * SIDE]
        total = ins[0][...].astype(jnp.float32)
        for part in ins[1:]:
            total = total + part[...].astype(jnp.float32)
        out_ref[:, lanes] = total.astype(jnp.bfloat16)


def add_rows(parts):
    rows, width = parts[0].shape
    return pl.pallas_call(
        add_rows_kernel,
        out_shape=jax.ShapeDtypeStruct((rows, PARTS * width), jnp.bfloat16),
        in_specs=whole(len(parts)),
        compiler_params=pltpu.CompilerParams(vmem_limit_bytes=8 << 20),
        name="add_rows",
    )(*parts)


def step(queries, probes, keys, values, w_out):
    core = lax.axis_index("c")
    first = core == 0
    table = table_of(lax.axis_index("x"), lax.axis_index("z"), core)
    wide = lax.all_gather(w_out, "y", axis=1, tiled=True)

    own_query, send_query = split_query(table, queries)
    got_query = swap(send_query)
    chip_query = jnp.where(
        first,
        jnp.concatenate([own_query, got_query], 1),
        jnp.concatenate([got_query, own_query], 1),
    )
    lines = [chip_query]
    for s in (1, 2, 3):
        lines.append(send(chip_query, "b", s))

    send_keys, send_values = other_half(table, keys, values)
    other_keys, other_values = swap(send_keys), swap(send_values)

    where = {}
    spread = spread_query(table, lines)
    for g, ks in enumerate(GROUPS):
        sources = [spread[g * SIDE]]
        for s in SHIFTS:
            sources.append(send(spread[g * SIDE + s], "a", s))
        for k in ks:
            where[k] = (ks[0], sources)

    head_probes = jnp.transpose(probes, (1, 2, 0))
    parts = []
    for call, sizes in CALLS:
        group, sources = where[call // SIDE]
        pieces = attend(
            table, call, sizes, group, sources, keys, other_keys, values, other_values, head_probes
        )
        for size, part in zip(sizes, pieces):
            if call // SIDE < SIDE - 1:
                part = send(part, "a", call // SIDE + 1)
            parts.append(part)
            call = call + size
    wide, parts[-1] = lax.optimization_barrier((wide, parts[-1]))
    got_wide = swap(wide)
    merged = combine(parts)
    passed = [merged[0]]
    for t in (1, 2, 3):
        passed.append(send(merged[t], "b", t))
    own_rows, send_rows = finish(table, passed)
    got_rows = swap(send_rows)

    projected = [project(n, own_rows, got_rows, wide, got_wide) for n in range(PARTS)]
    gathered = []
    for groups in projected:
        arrived = [groups[3]]
        for s in SHIFTS:
            arrived.append(send(groups[s - 1], "a", s))
        gathered.append(arrived)
    last = []
    for arrived in gathered:
        summed = add_lines(arrived)
        last.append(summed[0])
        for t in SHIFTS:
            last.append(send(summed[t], "b", t))
    return add_rows(last)


def solution(mesh):
    fine = Mesh(mesh.devices.reshape(4, SIDE, SIDE, 2), ("y",) + MEM)
    placed = (
        P(("y",) + MEM, None),
        P("y", None, None),
        P("y", MEM, None),
        P("y", MEM, None),
        P(MEM, "y"),
    )
    return jax.shard_map(
        step, mesh=fine, in_specs=placed, out_specs=P(("y",) + MEM, None), check_vma=False
    )
```

```python
import functools

import jax
import jax.numpy as jnp
from jax import lax
from jax.experimental import pallas as pl
from jax.experimental.pallas import tpu as pltpu
from jax.sharding import Mesh
from jax.sharding import PartitionSpec as P


DH = 128
BLOCK = 256
PAIR = 2 * DH
SIDE = 4
CHIPS = SIDE * SIDE
ROWS = 512
KEYS = 512
CHIP_ROWS = ROWS // CHIPS
CORE_ROWS = CHIP_ROWS // 2
STAT = 16
UNIT = 256
CHUNK = 64
PARTS = 2
PART = PAIR + STAT
NEG = -1e30
SCALE = DH ** -0.5 * 1.4426950408889634

MEM = ("x", "z", "c")
GROUPS = ((0,), (1,), (2, 3))
CALLS = ((0, 0, 4), (1, 0, 4), (2, 0, 4), (3, 0, 4))
SHIFTS = (1, 2, 3)
STEPS = (2, 1, 3, 0)
SWAP = [(0, 1), (1, 0)]

CORE = 0
BLOCKS = 1
PAIRS = 5
OTHER_PAIRS = PAIRS + CHIPS
ROW_AT = OTHER_PAIRS + CHIPS
MY_A = ROW_AT + CHIPS
MY_B = MY_A + 1


def shift(axis, step):
    moves = []
    for x in range(SIDE):
        for z in range(SIDE):
            for c in range(2):
                along_z = (axis == "a") == (c == 0)
                to_x = x if along_z else (x + step) % SIDE
                to_z = (z + step) % SIDE if along_z else z
                moves.append(((x * SIDE + z) * 2 + c, (to_x * SIDE + to_z) * 2 + c))
    return moves


def send(value, axis, step):
    return lax.ppermute(value, MEM, shift(axis, step))


def swap(value):
    return lax.ppermute(value, "c", SWAP)


def table_of(x, z, core):
    a = jnp.where(core == 0, z, x)
    b = jnp.where(core == 0, x, z)
    major = jnp.arange(CHIPS, dtype=jnp.int32) // SIDE
    minor = jnp.arange(CHIPS, dtype=jnp.int32) % SIDE
    step = jnp.where(major == 0, STEPS[0], jnp.where(major == 1, STEPS[1], jnp.where(major == 2, STEPS[2], 0)))

    def chip_at(along_a, along_b, on_core):
        return jnp.where(on_core == 0, along_b * SIDE + along_a, along_a * SIDE + along_b)

    own_block = ((x * SIDE + z) * 2 + core) * 2
    other_block = ((x * SIDE + z) * 2 + 1 - core) * 2
    blocks = jnp.where(jnp.arange(4) < 2, own_block, other_block) + jnp.arange(4) % 2
    pairs = chip_at((a + step) % SIDE, (b + minor) % SIDE, core)
    other_pairs = chip_at((b + step) % SIDE, (a + minor) % SIDE, 1 - core)
    row_at = chip_at((a + SIDE - major) % SIDE, minor, core) * CHIP_ROWS
    parts = [core.reshape(1), blocks, pairs, other_pairs, row_at, a.reshape(1), b.reshape(1)]
    return jnp.concatenate([p.astype(jnp.int32) for p in parts])


def whole(count):
    return [pl.BlockSpec(memory_space=pltpu.VMEM)] * count


def split_query_kernel(table, q_ref, own_ref, other_ref):
    first = table[CORE] == 0
    for p in range(CHIPS):
        turned = (p % SIDE) * SIDE + p // SIDE
        zero = q_ref[:, 2 * turned * PAIR:(2 * turned + 1) * PAIR]
        one = q_ref[:, (2 * p + 1) * PAIR:(2 * p + 2) * PAIR]
        here = pl.ds((p % SIDE) * PAIR, PAIR)
        own_ref[p // SIDE, :, here] = jnp.where(first, zero, one)
        other_ref[p // SIDE, :, here] = jnp.where(first, one, zero)


def split_query(table, queries):
    rows = queries.shape[0]
    half = jax.ShapeDtypeStruct((SIDE, rows, SIDE * PAIR), queries.dtype)
    return pl.pallas_call(
        split_query_kernel,
        out_shape=(half, half),
        in_specs=[pl.BlockSpec(memory_space=pltpu.SMEM)] + whole(1),
        compiler_params=pltpu.CompilerParams(vmem_limit_bytes=8 << 20),
        name="split_query",
    )(table, queries)


def spread_query_kernel(table, *refs):
    lines, outs = refs[:SIDE], refs[SIDE:]
    a, b = table[MY_A], table[MY_B]
    for t in range(SIDE):
        at = pl.ds(pl.multiple_of(((b + SIDE - t) % SIDE) * CHIP_ROWS, CHIP_ROWS), CHIP_ROWS)
        for g, ks in enumerate(GROUPS):
            for s in range(SIDE):
                for i, k in enumerate(ks):
                    group = (a + s + STEPS[k]) % SIDE
                    outs[g * SIDE + s][i, at, :] = lines[t][group]


def spread_query(table, lines):
    pieces = [
        jax.ShapeDtypeStruct((len(ks), SIDE * CHIP_ROWS, SIDE * PAIR), lines[0].dtype)
        for ks in GROUPS
        for _ in range(SIDE)
    ]
    return pl.pallas_call(
        spread_query_kernel,
        out_shape=tuple(pieces),
        in_specs=[pl.BlockSpec(memory_space=pltpu.SMEM)] + whole(SIDE),
        compiler_params=pltpu.CompilerParams(vmem_limit_bytes=16 << 20),
        name="spread_query",
    )(table, *lines)


def other_half_kernel(table, *refs):
    del table
    ins, outs = refs[:2 * SIDE], refs[2 * SIDE:]
    for n, out in enumerate(outs):
        for j in range(SIDE):
            out[:, j * PAIR:(j + 1) * PAIR] = ins[n * SIDE + j][0]


def other_half(table, keys, values):
    half = jax.ShapeDtypeStruct((KEYS, CHIPS * PAIR), keys.dtype)

    def source(j):
        return pl.BlockSpec(
            (1, KEYS, PAIR), lambda i, table: (0, 0, 2 * (i * SIDE + j) + 1 - table[CORE])
        )

    return pl.pallas_call(
        other_half_kernel,
        out_shape=(half, half),
        grid_spec=pltpu.PrefetchScalarGridSpec(
            num_scalar_prefetch=1,
            grid=(SIDE,),
            in_specs=[source(j) for j in range(SIDE)] * 2,
            out_specs=(pl.BlockSpec((KEYS, SIDE * PAIR), lambda i, table: (0, i)),) * 2,
        ),
        name="other_half",
    )(table, *[keys] * SIDE, *[values] * SIDE)


def attend_kernel(
    table, q0, q1, q2, q3, ka_ref, kb_ref, va_ref, vb_ref, probe_ref, out_ref,
    q_ref, s_ref, p_ref, v_ref, *, call, place,
):
    pair = table[PAIRS + call + pl.program_id(0)]
    turn = (table[MY_B] + call + pl.program_id(0)) % SIDE
    columns = pl.ds(pl.multiple_of(turn * PAIR, PAIR), PAIR)
    for s, source in enumerate((q0, q1, q2, q3)):
        for b in range(SIDE):
            at = pl.multiple_of(table[ROW_AT + s * SIDE + b], CHIP_ROWS)
            q_ref[pl.ds(at, CHIP_ROWS), :] = source[place, b * CHIP_ROWS:(b + 1) * CHIP_ROWS, columns]
    probe_at = 2 * pair + table[CORE]

    def other_lanes(h):
        return pl.ds(pl.multiple_of(pair * PAIR + h * DH, DH), DH)

    v_ref[:, :, DH:, :] = jnp.ones((2, 2, STAT, KEYS), jnp.bfloat16)

    units = [(h, r) for h in range(2) for r in range(ROWS // UNIT)]
    stat_row = lax.broadcasted_iota(jnp.int32, (STAT, UNIT), 0)
    stats = [jnp.zeros((STAT, UNIT), jnp.float32) for _ in range(ROWS // UNIT)]

    def block_tops(u, b):
        h, r = units[u]
        lanes = pl.ds(h * DH, DH)
        span = pl.ds((b % 2) * BLOCK, BLOCK)
        key = ka_ref[0, span, lanes] if b < 2 else kb_ref[span, other_lanes(h)]
        score = lax.dot_general(
            key, q_ref[r * UNIT:(r + 1) * UNIT, lanes], (((1,), (1,)), ((), ())),
            preferred_element_type=jnp.float32,
        )
        s_ref[u % 2, b] = score
        return jnp.max(score.reshape(-1, 8, UNIT), axis=0)

    def offsets(u, tops):
        h, r = units[u]
        probe = probe_ref[2 * probe_at + h, :, r * UNIT:(r + 1) * UNIT]
        top = jnp.full((1, UNIT), NEG, jnp.float32)
        hits = []
        for b in range(4):
            hit = jnp.max(jnp.where(probe == table[BLOCKS + b], 1.0, 0.0), axis=0, keepdims=True) > 0.5
            top = jnp.maximum(top, jnp.where(hit, jnp.max(tops[b], axis=0, keepdims=True), NEG))
            hits.append(hit)
        top = (top * SCALE).astype(jnp.bfloat16).astype(jnp.float32)
        return top, [jnp.where(hit, top, -NEG) for hit in hits]

    tops = [block_tops(0, b) for b in range(4)]
    for u, (h, r) in enumerate(units):
        top, offset = offsets(u, tops)
        tops = []
        lanes = pl.ds(h * DH, DH)
        if r == 0:
            v_ref[h, 0, :DH, :] = jnp.transpose(va_ref[0, :, lanes])
            v_ref[h, 1, :DH, :] = jnp.transpose(vb_ref[:, other_lanes(h)])
        for b in range(4):
            if u + 1 < len(units):
                tops.append(block_tops(u + 1, b))
            for c in range(0, BLOCK, CHUNK):
                weight = jnp.exp2(s_ref[u % 2, b, c:c + CHUNK, :] * SCALE - offset[b])
                p_ref[u % 2, b * BLOCK + c:b * BLOCK + c + CHUNK, :] = weight.astype(jnp.bfloat16)
        sums = jnp.dot(
            v_ref[h, 0], p_ref[u % 2, :KEYS, :], preferred_element_type=jnp.float32
        ) + jnp.dot(v_ref[h, 1], p_ref[u % 2, KEYS:, :], preferred_element_type=jnp.float32)
        out_ref[0, h * DH:(h + 1) * DH, r * UNIT:(r + 1) * UNIT] = sums[:DH].astype(jnp.bfloat16)
        total = sums[DH:DH + 1]
        high = total.astype(jnp.bfloat16).astype(jnp.float32)
        for j, row in enumerate((top, high, total - high)):
            stats[r] = jnp.where(stat_row == 3 * h + j, row, stats[r])
    for r, rows in enumerate(stats):
        out_ref[0, PAIR:, r * UNIT:(r + 1) * UNIT] = rows.astype(jnp.bfloat16)


def attend(table, k, start, count, place, sources, keys, other_keys, values, other_values, probes):
    own = pl.BlockSpec(
        (1, KEYS, PAIR),
        lambda j, table: (0, 0, 2 * table[PAIRS + k * SIDE + start + j] + table[CORE]),
    )
    here = pl.BlockSpec(memory_space=pltpu.VMEM)
    return pl.pallas_call(
        functools.partial(attend_kernel, call=k * SIDE + start, place=place),
        out_shape=jax.ShapeDtypeStruct((count, PART, ROWS), jnp.bfloat16),
        grid_spec=pltpu.PrefetchScalarGridSpec(
            num_scalar_prefetch=1,
            grid=(count,),
            in_specs=[here] * SIDE + [own, here, own, here, here],
            out_specs=pl.BlockSpec((1, PART, ROWS), lambda j, table: (j, 0, 0)),
            scratch_shapes=[
                pltpu.VMEM((ROWS, PAIR), jnp.bfloat16),
                pltpu.VMEM((2, 4, BLOCK, UNIT), jnp.float32),
                pltpu.VMEM((2, 2 * KEYS, UNIT), jnp.bfloat16),
                pltpu.VMEM((2, 2, DH + STAT, KEYS), jnp.bfloat16),
            ],
        ),
        compiler_params=pltpu.CompilerParams(vmem_limit_bytes=40 << 20),
    )(table, *sources, keys, other_keys, values, other_values, probes)


def merge(parts, h):
    tops = [part[PAIR + 3 * h:PAIR + 3 * h + 1, :].astype(jnp.float32) for part in parts]
    top = tops[0]
    for other in tops[1:]:
        top = jnp.maximum(top, other)
    total = jnp.zeros_like(top)
    numerator = jnp.zeros((DH, top.shape[1]), jnp.float32)
    for part, part_top in zip(parts, tops):
        scale = jnp.exp2(part_top - top)
        high = part[PAIR + 3 * h + 1:PAIR + 3 * h + 2, :].astype(jnp.float32)
        low = part[PAIR + 3 * h + 2:PAIR + 3 * h + 3, :].astype(jnp.float32)
        total = total + scale * (high + low)
        numerator = numerator + scale * part[h * DH:(h + 1) * DH, :].astype(jnp.float32)
    return top, total, numerator


def stat_rows(stats, h, top, total):
    stat_row = lax.broadcasted_iota(jnp.int32, stats.shape, 0)
    high = total.astype(jnp.bfloat16).astype(jnp.float32)
    for j, row in enumerate((top, high, total - high)):
        stats = jnp.where(stat_row == 3 * h + j, row, stats)
    return stats


def combine_kernel(*refs):
    ins, outs = refs[:-SIDE], refs[-SIDE:]
    lines = [[] for _ in range(SIDE)]
    at = 0
    for ref in ins:
        for i in range(ref.shape[0]):
            lines[at % SIDE].append(ref.at[i])
            at += 1
    for parts, out in zip(lines, outs):
        stats = jnp.zeros((STAT, ROWS), jnp.float32)
        for h in range(2):
            top, total, numerator = merge(parts, h)
            out[h * DH:(h + 1) * DH, :] = numerator.astype(jnp.bfloat16)
            stats = stat_rows(stats, h, top, total)
        out[PAIR:, :] = stats.astype(jnp.bfloat16)


def combine(parts):
    return pl.pallas_call(
        combine_kernel,
        out_shape=(jax.ShapeDtypeStruct((PART, ROWS), jnp.bfloat16),) * SIDE,
        in_specs=whole(len(parts)),
        compiler_params=pltpu.CompilerParams(vmem_limit_bytes=16 << 20),
        name="combine",
    )(*parts)


def finish_kernel(table, *refs):
    ins, own_ref, other_ref, rows_ref = refs[:SIDE], refs[SIDE], refs[SIDE + 1], refs[SIDE + 2]
    for h in range(2):
        _, total, numerator = merge(ins, h)
        rows_ref[:, h * DH:(h + 1) * DH] = jnp.transpose(numerator / total).astype(jnp.bfloat16)
    for ref, at, core in ((own_ref, PAIRS, table[CORE]), (other_ref, OTHER_PAIRS, 1 - table[CORE])):
        for p in range(CHIPS):
            start = pl.multiple_of(table[at + p] * CHIP_ROWS + core * CORE_ROWS, CORE_ROWS)
            ref[p] = rows_ref[pl.ds(start, CORE_ROWS), :]


def finish(table, parts):
    rows = jax.ShapeDtypeStruct((CHIPS, CORE_ROWS, PAIR), jnp.bfloat16)
    return pl.pallas_call(
        finish_kernel,
        out_shape=(rows, rows),
        in_specs=[pl.BlockSpec(memory_space=pltpu.SMEM)] + whole(SIDE),
        scratch_shapes=[pltpu.VMEM((ROWS, PAIR), jnp.bfloat16)],
        compiler_params=pltpu.CompilerParams(vmem_limit_bytes=12 << 20),
        name="finish",
    )(table, *parts)


def project_kernel(own_ref, got_ref, own_w_ref, got_w_ref, *outs):
    own = own_ref[...].reshape(-1, PAIR)
    got = got_ref[...].reshape(-1, PAIR)
    step = 256
    for n in range(own_w_ref.shape[1] // step):
        lanes = pl.ds(n * step, step)
        result = jnp.dot(own, own_w_ref[:, lanes], preferred_element_type=jnp.float32)
        result = result + jnp.dot(got, got_w_ref[:, lanes], preferred_element_type=jnp.float32)
        result = result.astype(jnp.bfloat16).reshape(len(outs), SIDE, CORE_ROWS, step)
        for g, out in enumerate(outs):
            out[:, :, lanes] = result[g]


def project(part, own, got, own_w, got_w):
    width = got_w.shape[1] // PARTS
    rows = pl.BlockSpec((CHIPS, CORE_ROWS, PAIR), lambda i: (0, 0, 0))
    weight = pl.BlockSpec((PAIR, width), lambda i: (0, part), pipeline_mode=pl.Buffered(1))
    out = jax.ShapeDtypeStruct((SIDE, CORE_ROWS, width), jnp.bfloat16)
    return pl.pallas_call(
        project_kernel,
        out_shape=(out,) * SIDE,
        grid=(1,),
        in_specs=[rows, rows, weight, weight],
        out_specs=(pl.BlockSpec((SIDE, CORE_ROWS, width), lambda i: (0, 0, 0)),) * SIDE,
        compiler_params=pltpu.CompilerParams(vmem_limit_bytes=24 << 20),
    )(own, got, own_w, got_w)


def add_lines_kernel(*refs):
    ins, outs = refs[:SIDE], refs[SIDE:]
    for t, out in enumerate(outs):
        total = ins[0][t].astype(jnp.float32)
        for ref in ins[1:]:
            total = total + ref[t].astype(jnp.float32)
        out[...] = total.astype(jnp.bfloat16)


def add_lines(parts):
    width = parts[0].shape[2]
    return pl.pallas_call(
        add_lines_kernel,
        out_shape=(jax.ShapeDtypeStruct((CORE_ROWS, width), jnp.bfloat16),) * SIDE,
        in_specs=whole(SIDE),
        compiler_params=pltpu.CompilerParams(vmem_limit_bytes=8 << 20),
        name="add_lines",
    )(*parts)


def add_rows_kernel(*refs):
    out_ref = refs[-1]
    width = out_ref.shape[1] // PARTS
    for n in range(PARTS):
        lanes = pl.ds(n * width, width)
        ins = refs[n * SIDE:(n + 1) * SIDE]
        total = ins[0][...].astype(jnp.float32)
        for part in ins[1:]:
            total = total + part[...].astype(jnp.float32)
        out_ref[:, lanes] = total.astype(jnp.bfloat16)


def add_rows(parts):
    rows, width = parts[0].shape
    return pl.pallas_call(
        add_rows_kernel,
        out_shape=jax.ShapeDtypeStruct((rows, PARTS * width), jnp.bfloat16),
        in_specs=whole(len(parts)),
        compiler_params=pltpu.CompilerParams(vmem_limit_bytes=8 << 20),
        name="add_rows",
    )(*parts)


def step(queries, probes, keys, values, w_out):
    core = lax.axis_index("c")
    first = core == 0
    table = table_of(lax.axis_index("x"), lax.axis_index("z"), core)
    wide = lax.all_gather(w_out, "y", axis=1, tiled=True)

    own_query, send_query = split_query(table, queries)
    got_query = swap(send_query)
    chip_query = jnp.where(
        first,
        jnp.concatenate([own_query, got_query], 1),
        jnp.concatenate([got_query, own_query], 1),
    )
    lines = [chip_query]
    for s in (1, 2, 3):
        lines.append(send(chip_query, "b", s))

    send_keys, send_values = other_half(table, keys, values)
    other_keys, other_values = swap(send_keys), swap(send_values)

    where = {}
    spread = spread_query(table, lines)
    for g, ks in enumerate(GROUPS):
        sources = [spread[g * SIDE]]
        for s in SHIFTS:
            sources.append(send(spread[g * SIDE + s], "a", s))
        for i, k in enumerate(ks):
            where[k] = (i, sources)

    head_probes = jnp.transpose(probes, (1, 2, 0))
    parts = []
    for k, start, count in CALLS:
        place, sources = where[k]
        part = attend(
            table, k, start, count, place, sources, keys, other_keys, values, other_values, head_probes
        )
        if k < SIDE - 1:
            part = send(part, "a", STEPS[k])
        parts.append(part)
    wide, parts[-1] = lax.optimization_barrier((wide, parts[-1]))
    got_wide = swap(wide)
    merged = combine(parts)
    passed = [merged[0]]
    for t in (1, 2, 3):
        passed.append(send(merged[t], "b", t))
    own_rows, send_rows = finish(table, passed)
    got_rows = swap(send_rows)

    projected = [project(n, own_rows, got_rows, wide, got_wide) for n in range(PARTS)]
    gathered = []
    for groups in projected:
        arrived = [groups[3]]
        for s in SHIFTS:
            arrived.append(send(groups[STEPS.index(s)], "a", s))
        gathered.append(arrived)
    last = []
    for arrived in gathered:
        summed = add_lines(arrived)
        last.append(summed[0])
        for t in SHIFTS:
            last.append(send(summed[t], "b", t))
    return add_rows(last)


def solution(mesh):
    fine = Mesh(mesh.devices.reshape(4, SIDE, SIDE, 2), ("y",) + MEM)
    placed = (
        P(("y",) + MEM, None),
        P("y", None, None),
        P("y", MEM, None),
        P("y", MEM, None),
        P(MEM, "y"),
    )
    return jax.shard_map(
        step, mesh=fine, in_specs=placed, out_specs=P(("y",) + MEM, None), check_vma=False
    )
```

```python
import functools

import jax
import jax.numpy as jnp
from jax import lax
from jax.experimental import pallas as pl
from jax.experimental.pallas import tpu as pltpu
from jax.sharding import Mesh
from jax.sharding import PartitionSpec as P


DH = 128
BLOCK = 256
PAIR = 2 * DH
SIDE = 4
CHIPS = SIDE * SIDE
ROWS = 512
KEYS = 512
CHIP_ROWS = ROWS // CHIPS
CORE_ROWS = CHIP_ROWS // 2
STAT = 16
UNIT = 256
CHUNK = 64
PARTS = 2
PART = PAIR + STAT
NEG = -1e30
SCALE = DH ** -0.5 * 1.4426950408889634

MEM = ("x", "z", "c")
GROUPS = ((0,), (1, 2), (3,))
CALLS = ((0, (4,)), (4, (4, 2)), (10, (2,)), (12, (4,)))
SHIFTS = (1, 2, 3)
STEPS = (2, 1, 3, 0)
SWAP = [(0, 1), (1, 0)]

CORE = 0
BLOCKS = 1
PAIRS = 5
OTHER_PAIRS = PAIRS + CHIPS
ROW_AT = OTHER_PAIRS + CHIPS
MY_A = ROW_AT + CHIPS
MY_B = MY_A + 1


def shift(axis, step):
    moves = []
    for x in range(SIDE):
        for z in range(SIDE):
            for c in range(2):
                along_z = (axis == "a") == (c == 0)
                to_x = x if along_z else (x + step) % SIDE
                to_z = (z + step) % SIDE if along_z else z
                moves.append(((x * SIDE + z) * 2 + c, (to_x * SIDE + to_z) * 2 + c))
    return moves


def send(value, axis, step):
    return lax.ppermute(value, MEM, shift(axis, step))


def swap(value):
    return lax.ppermute(value, "c", SWAP)


def table_of(x, z, core):
    a = jnp.where(core == 0, z, x)
    b = jnp.where(core == 0, x, z)
    major = jnp.arange(CHIPS, dtype=jnp.int32) // SIDE
    minor = jnp.arange(CHIPS, dtype=jnp.int32) % SIDE
    step = jnp.where(major == 0, STEPS[0], jnp.where(major == 1, STEPS[1], jnp.where(major == 2, STEPS[2], 0)))

    def chip_at(along_a, along_b, on_core):
        return jnp.where(on_core == 0, along_b * SIDE + along_a, along_a * SIDE + along_b)

    own_block = ((x * SIDE + z) * 2 + core) * 2
    other_block = ((x * SIDE + z) * 2 + 1 - core) * 2
    blocks = jnp.where(jnp.arange(4) < 2, own_block, other_block) + jnp.arange(4) % 2
    pairs = chip_at((a + step) % SIDE, (b + minor) % SIDE, core)
    other_pairs = chip_at((b + step) % SIDE, (a + minor) % SIDE, 1 - core)
    row_at = chip_at((a + SIDE - major) % SIDE, minor, core) * CHIP_ROWS
    parts = [core.reshape(1), blocks, pairs, other_pairs, row_at, a.reshape(1), b.reshape(1)]
    return jnp.concatenate([p.astype(jnp.int32) for p in parts])


def whole(count):
    return [pl.BlockSpec(memory_space=pltpu.VMEM)] * count


def split_query_kernel(table, q_ref, own_ref, other_ref):
    first = table[CORE] == 0
    for p in range(CHIPS):
        turned = (p % SIDE) * SIDE + p // SIDE
        zero = q_ref[:, 2 * turned * PAIR:(2 * turned + 1) * PAIR]
        one = q_ref[:, (2 * p + 1) * PAIR:(2 * p + 2) * PAIR]
        here = pl.ds((p % SIDE) * PAIR, PAIR)
        own_ref[p // SIDE, :, here] = jnp.where(first, zero, one)
        other_ref[p // SIDE, :, here] = jnp.where(first, one, zero)


def split_query(table, queries):
    rows = queries.shape[0]
    half = jax.ShapeDtypeStruct((SIDE, rows, SIDE * PAIR), queries.dtype)
    return pl.pallas_call(
        split_query_kernel,
        out_shape=(half, half),
        in_specs=[pl.BlockSpec(memory_space=pltpu.SMEM)] + whole(1),
        compiler_params=pltpu.CompilerParams(vmem_limit_bytes=8 << 20),
        name="split_query",
    )(table, queries)


def spread_query_kernel(table, *refs):
    lines, outs = refs[:SIDE], refs[SIDE:]
    a, b = table[MY_A], table[MY_B]
    for t in range(SIDE):
        at = pl.ds(pl.multiple_of(((b + SIDE - t) % SIDE) * CHIP_ROWS, CHIP_ROWS), CHIP_ROWS)
        for g, ks in enumerate(GROUPS):
            for s in range(SIDE):
                for i, k in enumerate(ks):
                    group = (a + s + STEPS[k]) % SIDE
                    outs[g * SIDE + s][i, at, :] = lines[t][group]


def spread_query(table, lines):
    pieces = [
        jax.ShapeDtypeStruct((len(ks), SIDE * CHIP_ROWS, SIDE * PAIR), lines[0].dtype)
        for ks in GROUPS
        for _ in range(SIDE)
    ]
    return pl.pallas_call(
        spread_query_kernel,
        out_shape=tuple(pieces),
        in_specs=[pl.BlockSpec(memory_space=pltpu.SMEM)] + whole(SIDE),
        compiler_params=pltpu.CompilerParams(vmem_limit_bytes=16 << 20),
        name="spread_query",
    )(table, *lines)


def other_half_kernel(table, *refs):
    del table
    ins, outs = refs[:2 * SIDE], refs[2 * SIDE:]
    for n, out in enumerate(outs):
        for j in range(SIDE):
            out[:, j * PAIR:(j + 1) * PAIR] = ins[n * SIDE + j][0]


def other_half(table, keys, values):
    half = jax.ShapeDtypeStruct((KEYS, CHIPS * PAIR), keys.dtype)

    def source(j):
        return pl.BlockSpec(
            (1, KEYS, PAIR), lambda i, table: (0, 0, 2 * (i * SIDE + j) + 1 - table[CORE])
        )

    return pl.pallas_call(
        other_half_kernel,
        out_shape=(half, half),
        grid_spec=pltpu.PrefetchScalarGridSpec(
            num_scalar_prefetch=1,
            grid=(SIDE,),
            in_specs=[source(j) for j in range(SIDE)] * 2,
            out_specs=(pl.BlockSpec((KEYS, SIDE * PAIR), lambda i, table: (0, i)),) * 2,
        ),
        name="other_half",
    )(table, *[keys] * SIDE, *[values] * SIDE)


def attend_kernel(
    table, q0, q1, q2, q3, ka_ref, kb_ref, va_ref, vb_ref, probe_ref, *refs, call, group, sizes
):
    outs = refs[:len(sizes)]
    q_ref, s_ref, p_ref, v_ref, o_ref = refs[len(sizes):]
    place = (call + pl.program_id(0)) // SIDE - group
    out_ref = o_ref if len(sizes) > 1 else outs[0]
    pair = table[PAIRS + call + pl.program_id(0)]
    turn = (table[MY_B] + call + pl.program_id(0)) % SIDE
    columns = pl.ds(pl.multiple_of(turn * PAIR, PAIR), PAIR)
    for s, source in enumerate((q0, q1, q2, q3)):
        for b in range(SIDE):
            at = pl.multiple_of(table[ROW_AT + s * SIDE + b], CHIP_ROWS)
            q_ref[pl.ds(at, CHIP_ROWS), :] = source[place, b * CHIP_ROWS:(b + 1) * CHIP_ROWS, columns]
    probe_at = 2 * pair + table[CORE]

    def other_lanes(h):
        return pl.ds(pl.multiple_of(pair * PAIR + h * DH, DH), DH)

    v_ref[:, :, DH:, :] = jnp.ones((2, 2, STAT, KEYS), jnp.bfloat16)

    units = [(h, r) for h in range(2) for r in range(ROWS // UNIT)]
    stat_row = lax.broadcasted_iota(jnp.int32, (STAT, UNIT), 0)
    stats = [jnp.zeros((STAT, UNIT), jnp.float32) for _ in range(ROWS // UNIT)]

    def block_tops(u, b):
        h, r = units[u]
        lanes = pl.ds(h * DH, DH)
        span = pl.ds((b % 2) * BLOCK, BLOCK)
        key = ka_ref[0, span, lanes] if b < 2 else kb_ref[span, other_lanes(h)]
        score = lax.dot_general(
            key, q_ref[r * UNIT:(r + 1) * UNIT, lanes], (((1,), (1,)), ((), ())),
            preferred_element_type=jnp.float32,
        )
        s_ref[u % 2, b] = score
        return jnp.max(score.reshape(-1, 8, UNIT), axis=0)

    def offsets(u, tops):
        h, r = units[u]
        probe = probe_ref[2 * probe_at + h, :, r * UNIT:(r + 1) * UNIT]
        top = jnp.full((1, UNIT), NEG, jnp.float32)
        hits = []
        for b in range(4):
            hit = jnp.max(jnp.where(probe == table[BLOCKS + b], 1.0, 0.0), axis=0, keepdims=True) > 0.5
            top = jnp.maximum(top, jnp.where(hit, jnp.max(tops[b], axis=0, keepdims=True), NEG))
            hits.append(hit)
        top = (top * SCALE).astype(jnp.bfloat16).astype(jnp.float32)
        return top, [jnp.where(hit, top, -NEG) for hit in hits]

    tops = [block_tops(0, b) for b in range(4)]
    for u, (h, r) in enumerate(units):
        top, offset = offsets(u, tops)
        tops = []
        lanes = pl.ds(h * DH, DH)
        if r == 0:
            v_ref[h, 0, :DH, :] = jnp.transpose(va_ref[0, :, lanes])
            v_ref[h, 1, :DH, :] = jnp.transpose(vb_ref[:, other_lanes(h)])
        for b in range(4):
            if u + 1 < len(units):
                tops.append(block_tops(u + 1, b))
            for c in range(0, BLOCK, CHUNK):
                weight = jnp.exp2(s_ref[u % 2, b, c:c + CHUNK, :] * SCALE - offset[b])
                p_ref[u % 2, b * BLOCK + c:b * BLOCK + c + CHUNK, :] = weight.astype(jnp.bfloat16)
        sums = jnp.dot(
            v_ref[h, 0], p_ref[u % 2, :KEYS, :], preferred_element_type=jnp.float32
        ) + jnp.dot(v_ref[h, 1], p_ref[u % 2, KEYS:, :], preferred_element_type=jnp.float32)
        out_ref[0, h * DH:(h + 1) * DH, r * UNIT:(r + 1) * UNIT] = sums[:DH].astype(jnp.bfloat16)
        total = sums[DH:DH + 1]
        high = total.astype(jnp.bfloat16).astype(jnp.float32)
        for j, row in enumerate((top, high, total - high)):
            stats[r] = jnp.where(stat_row == 3 * h + j, row, stats[r])
    for r, rows in enumerate(stats):
        out_ref[0, PAIR:, r * UNIT:(r + 1) * UNIT] = rows.astype(jnp.bfloat16)
    if len(sizes) > 1:
        step = pl.program_id(0)

        @pl.when(step < sizes[0])
        def _():
            outs[0][...] = o_ref[...]

        @pl.when(step >= sizes[0])
        def _():
            outs[1][...] = o_ref[...]


def attend(table, call, sizes, group, sources, keys, other_keys, values, other_values, probes):
    own = pl.BlockSpec(
        (1, KEYS, PAIR), lambda j, table: (0, 0, 2 * table[PAIRS + call + j] + table[CORE])
    )
    here = pl.BlockSpec(memory_space=pltpu.VMEM)
    spots = [lambda j, table: (jnp.minimum(j, sizes[0] - 1), 0, 0)]
    if len(sizes) > 1:
        spots.append(lambda j, table: (jnp.maximum(j - sizes[0], 0), 0, 0))
    return pl.pallas_call(
        functools.partial(attend_kernel, call=call, group=group, sizes=sizes),
        out_shape=tuple(jax.ShapeDtypeStruct((n, PART, ROWS), jnp.bfloat16) for n in sizes),
        grid_spec=pltpu.PrefetchScalarGridSpec(
            num_scalar_prefetch=1,
            grid=(sum(sizes),),
            in_specs=[here] * SIDE + [own, here, own, here, here],
            out_specs=tuple(pl.BlockSpec((1, PART, ROWS), spot) for spot in spots),
            scratch_shapes=[
                pltpu.VMEM((ROWS, PAIR), jnp.bfloat16),
                pltpu.VMEM((2, 4, BLOCK, UNIT), jnp.float32),
                pltpu.VMEM((2, 2 * KEYS, UNIT), jnp.bfloat16),
                pltpu.VMEM((2, 2, DH + STAT, KEYS), jnp.bfloat16),
                pltpu.VMEM((1, PART, ROWS), jnp.bfloat16),
            ],
        ),
        compiler_params=pltpu.CompilerParams(vmem_limit_bytes=40 << 20),
    )(table, *sources, keys, other_keys, values, other_values, probes)


def merge(parts, h):
    tops = [part[PAIR + 3 * h:PAIR + 3 * h + 1, :].astype(jnp.float32) for part in parts]
    top = tops[0]
    for other in tops[1:]:
        top = jnp.maximum(top, other)
    total = jnp.zeros_like(top)
    numerator = jnp.zeros((DH, top.shape[1]), jnp.float32)
    for part, part_top in zip(parts, tops):
        scale = jnp.exp2(part_top - top)
        high = part[PAIR + 3 * h + 1:PAIR + 3 * h + 2, :].astype(jnp.float32)
        low = part[PAIR + 3 * h + 2:PAIR + 3 * h + 3, :].astype(jnp.float32)
        total = total + scale * (high + low)
        numerator = numerator + scale * part[h * DH:(h + 1) * DH, :].astype(jnp.float32)
    return top, total, numerator


def stat_rows(stats, h, top, total):
    stat_row = lax.broadcasted_iota(jnp.int32, stats.shape, 0)
    high = total.astype(jnp.bfloat16).astype(jnp.float32)
    for j, row in enumerate((top, high, total - high)):
        stats = jnp.where(stat_row == 3 * h + j, row, stats)
    return stats


def combine_kernel(*refs):
    ins, outs = refs[:-SIDE], refs[-SIDE:]
    lines = [[] for _ in range(SIDE)]
    at = 0
    for ref in ins:
        for i in range(ref.shape[0]):
            lines[at % SIDE].append(ref.at[i])
            at += 1
    for parts, out in zip(lines, outs):
        stats = jnp.zeros((STAT, ROWS), jnp.float32)
        for h in range(2):
            top, total, numerator = merge(parts, h)
            out[h * DH:(h + 1) * DH, :] = numerator.astype(jnp.bfloat16)
            stats = stat_rows(stats, h, top, total)
        out[PAIR:, :] = stats.astype(jnp.bfloat16)


def combine(parts):
    return pl.pallas_call(
        combine_kernel,
        out_shape=(jax.ShapeDtypeStruct((PART, ROWS), jnp.bfloat16),) * SIDE,
        in_specs=whole(len(parts)),
        compiler_params=pltpu.CompilerParams(vmem_limit_bytes=16 << 20),
        name="combine",
    )(*parts)


def finish_kernel(table, *refs):
    ins, own_ref, other_ref, rows_ref = refs[:SIDE], refs[SIDE], refs[SIDE + 1], refs[SIDE + 2]
    for h in range(2):
        _, total, numerator = merge(ins, h)
        rows_ref[:, h * DH:(h + 1) * DH] = jnp.transpose(numerator / total).astype(jnp.bfloat16)
    for ref, at, core in ((own_ref, PAIRS, table[CORE]), (other_ref, OTHER_PAIRS, 1 - table[CORE])):
        for p in range(CHIPS):
            start = pl.multiple_of(table[at + p] * CHIP_ROWS + core * CORE_ROWS, CORE_ROWS)
            ref[p] = rows_ref[pl.ds(start, CORE_ROWS), :]


def finish(table, parts):
    rows = jax.ShapeDtypeStruct((CHIPS, CORE_ROWS, PAIR), jnp.bfloat16)
    return pl.pallas_call(
        finish_kernel,
        out_shape=(rows, rows),
        in_specs=[pl.BlockSpec(memory_space=pltpu.SMEM)] + whole(SIDE),
        scratch_shapes=[pltpu.VMEM((ROWS, PAIR), jnp.bfloat16)],
        compiler_params=pltpu.CompilerParams(vmem_limit_bytes=12 << 20),
        name="finish",
    )(table, *parts)


def project_kernel(own_ref, got_ref, own_w_ref, got_w_ref, *outs):
    own = own_ref[...].reshape(-1, PAIR)
    got = got_ref[...].reshape(-1, PAIR)
    step = 256
    for n in range(own_w_ref.shape[1] // step):
        lanes = pl.ds(n * step, step)
        result = jnp.dot(own, own_w_ref[:, lanes], preferred_element_type=jnp.float32)
        result = result + jnp.dot(got, got_w_ref[:, lanes], preferred_element_type=jnp.float32)
        result = result.astype(jnp.bfloat16).reshape(len(outs), SIDE, CORE_ROWS, step)
        for g, out in enumerate(outs):
            out[:, :, lanes] = result[g]


def project(part, own, got, own_w, got_w):
    width = got_w.shape[1] // PARTS
    rows = pl.BlockSpec((CHIPS, CORE_ROWS, PAIR), lambda i: (0, 0, 0))
    weight = pl.BlockSpec((PAIR, width), lambda i: (0, part), pipeline_mode=pl.Buffered(1))
    out = jax.ShapeDtypeStruct((SIDE, CORE_ROWS, width), jnp.bfloat16)
    return pl.pallas_call(
        project_kernel,
        out_shape=(out,) * SIDE,
        grid=(1,),
        in_specs=[rows, rows, weight, weight],
        out_specs=(pl.BlockSpec((SIDE, CORE_ROWS, width), lambda i: (0, 0, 0)),) * SIDE,
        compiler_params=pltpu.CompilerParams(vmem_limit_bytes=24 << 20),
    )(own, got, own_w, got_w)


def add_lines_kernel(*refs):
    ins, outs = refs[:SIDE], refs[SIDE:]
    for t, out in enumerate(outs):
        total = ins[0][t].astype(jnp.float32)
        for ref in ins[1:]:
            total = total + ref[t].astype(jnp.float32)
        out[...] = total.astype(jnp.bfloat16)


def add_lines(parts):
    width = parts[0].shape[2]
    return pl.pallas_call(
        add_lines_kernel,
        out_shape=(jax.ShapeDtypeStruct((CORE_ROWS, width), jnp.bfloat16),) * SIDE,
        in_specs=whole(SIDE),
        compiler_params=pltpu.CompilerParams(vmem_limit_bytes=8 << 20),
        name="add_lines",
    )(*parts)


def add_rows_kernel(*refs):
    out_ref = refs[-1]
    width = out_ref.shape[1] // PARTS
    for n in range(PARTS):
        lanes = pl.ds(n * width, width)
        ins = refs[n * SIDE:(n + 1) * SIDE]
        total = ins[0][...].astype(jnp.float32)
        for part in ins[1:]:
            total = total + part[...].astype(jnp.float32)
        out_ref[:, lanes] = total.astype(jnp.bfloat16)


def add_rows(parts):
    rows, width = parts[0].shape
    return pl.pallas_call(
        add_rows_kernel,
        out_shape=jax.ShapeDtypeStruct((rows, PARTS * width), jnp.bfloat16),
        in_specs=whole(len(parts)),
        compiler_params=pltpu.CompilerParams(vmem_limit_bytes=8 << 20),
        name="add_rows",
    )(*parts)


def step(queries, probes, keys, values, w_out):
    core = lax.axis_index("c")
    first = core == 0
    table = table_of(lax.axis_index("x"), lax.axis_index("z"), core)
    wide = lax.all_gather(w_out, "y", axis=1, tiled=True)

    own_query, send_query = split_query(table, queries)
    got_query = swap(send_query)
    chip_query = jnp.where(
        first,
        jnp.concatenate([own_query, got_query], 1),
        jnp.concatenate([got_query, own_query], 1),
    )
    lines = [chip_query]
    for s in (1, 2, 3):
        lines.append(send(chip_query, "b", s))

    send_keys, send_values = other_half(table, keys, values)
    other_keys, other_values = swap(send_keys), swap(send_values)

    where = {}
    spread = spread_query(table, lines)
    for g, ks in enumerate(GROUPS):
        sources = [spread[g * SIDE]]
        for s in SHIFTS:
            sources.append(send(spread[g * SIDE + s], "a", s))
        for k in ks:
            where[k] = (ks[0], sources)

    head_probes = jnp.transpose(probes, (1, 2, 0))
    parts = []
    for call, sizes in CALLS:
        group, sources = where[call // SIDE]
        pieces = attend(
            table, call, sizes, group, sources, keys, other_keys, values, other_values, head_probes
        )
        for size, part in zip(sizes, pieces):
            if call // SIDE < SIDE - 1:
                part = send(part, "a", STEPS[call // SIDE])
            parts.append(part)
            call = call + size
    wide, parts[-1] = lax.optimization_barrier((wide, parts[-1]))
    got_wide = swap(wide)
    merged = combine(parts)
    passed = [merged[0]]
    for t in (1, 2, 3):
        passed.append(send(merged[t], "b", t))
    own_rows, send_rows = finish(table, passed)
    got_rows = swap(send_rows)

    projected = [project(n, own_rows, got_rows, wide, got_wide) for n in range(PARTS)]
    gathered = []
    for groups in projected:
        arrived = [groups[3]]
        for s in SHIFTS:
            arrived.append(send(groups[STEPS.index(s)], "a", s))
        gathered.append(arrived)
    last = []
    for arrived in gathered:
        summed = add_lines(arrived)
        last.append(summed[0])
        for t in SHIFTS:
            last.append(send(summed[t], "b", t))
    return add_rows(last)


def solution(mesh):
    fine = Mesh(mesh.devices.reshape(4, SIDE, SIDE, 2), ("y",) + MEM)
    placed = (
        P(("y",) + MEM, None),
        P("y", None, None),
        P("y", MEM, None),
        P("y", MEM, None),
        P(MEM, "y"),
    )
    return jax.shard_map(
        step, mesh=fine, in_specs=placed, out_specs=P(("y",) + MEM, None), check_vma=False
    )
```
